512 devices in a mesh: blk: 32 (over z, y_hi), col: 16 (over x, y_lo, core).
Axes of the slice: x: 4, y: 8 (y_hi: 4, y_lo: 2; y = y_hi * 2 + y_lo), z: 8, core: 2. Of those that a mesh axis runs over, the one named last changes fastest.
Arguments:
- amps: bfloat16 [32, 16, 2, 128, 128], P('blk', 'col'), may hold values from -6 to 6
- driver: float32 [32, 16, 2, 128, 128], P('blk', 'col')
- pattern: int32 [32, 16, 2, 32, 2], P('blk', 'col'), may hold values from -1 to 31, as said below
- domain: int32 [32, 16, 2], P('blk', 'col'), may hold values from 32 to 128
- virt_energy: float32 [32, 16, 2, 128], P('blk', 'col'), may hold values from 0.5 to 4
- pair_gap: float32 [32, 16, 2], P('blk', 'col'), may hold values from 0.5 to 2
- integrals: bfloat16 [32, 128, 128], P('col'), may hold values from -0.0625 to 0.0625
Outputs:
- new_amps: float32 [32, 16, 2, 128, 128], P('blk', 'col')
- resid_rms: float32 [], replicated
The draws below stay inside these ranges and needn't reach their ends.
Inputs may be any that keep to these rules, and one draw needn't show every extreme that they name: `pattern`: about a third of the entries are -1; the others name integral tiles of all owners.
All inputs are finite; a program needn't handle non-finite values.
Results may differ from the reference program's by a relative error of at most 0.0003.
Values may be sent and summed in bfloat16 or wider, within the bound.
A program may use at most 64 MiB of HBM per device.

```python
import math
import jax
import jax.numpy as jnp
from jax import lax

V = 128
PD = 2
INT_DEV = 2
BLOCKS = 32
GROUPS = 16
NINT = 32


def draw_pattern(key, part):
    shape = (BLOCKS, GROUPS, PD, BLOCKS, PD)
    first, second = jax.random.split(key)
    tile_index = jax.random.randint(first, shape, 0, INT_DEV * GROUPS)
    keeper = jax.random.randint(second, shape, 0, 3)
    return jnp.where(keeper > 0, tile_index, -1).astype(jnp.int32)


def draw_driver(key, part):
    shape = (BLOCKS, GROUPS, PD, V, V)
    first = jax.random.fold_in(key, 0)
    place = (jnp.arange(BLOCKS)[:, None] * GROUPS + jnp.arange(GROUPS)[None, :]).astype(jnp.float32)
    place = place / float(max(BLOCKS * GROUPS - 1, 1))
    ramp = 0.5 + 1.5 * place
    base = jax.random.normal(first, shape, jnp.float32)
    return base * ramp[:, :, None, None, None]


def place_ends(entries, own_key, smallest, high):
    extent = entries.shape
    index_at = [jax.random.randint(jax.random.fold_in(own_key, axis), (), 0, extent[axis]) for axis in range(len(extent))]
    entries = entries.at[tuple(index_at)].set(smallest)
    longest = extent.index(max(extent))
    index_at[longest] = (index_at[longest] + 1) % extent[longest]
    return entries.at[tuple(index_at)].set(high)


def level_of(rng, dims, cuts, smallest, largest):
    gain = 1.0
    for dim, shards_of in cuts:
        heights = jax.random.uniform(jax.random.fold_in(jax.random.fold_in(rng, 6), dim), (shards_of,), jnp.float32, smallest / len(cuts), largest / len(cuts))
        gain = gain * jnp.repeat(jnp.exp(heights), dims[dim] // shards_of).reshape((-1,) + (1,) * (len(dims) - 1 - dim))
    return gain


def noise(rng, dims, scale, most, pieces=(), held_as=jnp.bfloat16):
    gain = level_of(rng, dims, pieces, -0.22, 0.18) if pieces else 1.0
    values = jax.random.normal(rng, dims, jnp.float32) * scale * gain
    return jnp.minimum(jnp.maximum(values, -most), most).astype(held_as)


def setup_inputs(seed: int = 0) -> dict:
    key_list = jax.random.split(jax.random.key(seed), 8)
    amps = noise(key_list[0], (BLOCKS, GROUPS, PD, V, V), 1.0, 6.0, ((0, 32), (1, 16)))
    driver = draw_driver(jax.random.fold_in(key_list[7], 71), 0)
    pattern = draw_pattern(jax.random.fold_in(key_list[7], 71), 0)
    domain = place_ends(jax.random.randint(key_list[3], (BLOCKS, GROUPS, PD), V // 4, V + 1), jax.random.fold_in(key_list[3], 1), V // 4, V).astype(jnp.int32)
    virt_energy = jnp.clip(jnp.exp(math.log(4.0) - 2.0794415 * jax.random.uniform(key_list[4], (BLOCKS, GROUPS, PD, V), jnp.float32) ** level_of(key_list[4], (BLOCKS, GROUPS, PD, V), ((0, 32), (1, 16)), -0.2, 0.2)), 0.5, 4.0)
    pair_gap = jnp.clip(jnp.exp(math.log(2.0) - 1.3862944 * jax.random.uniform(key_list[5], (BLOCKS, GROUPS, PD), jnp.float32) ** level_of(key_list[5], (BLOCKS, GROUPS, PD), ((0, 32), (1, 16)), -0.2, 0.2)), 0.5, 2.0)
    integrals = noise(key_list[6], (NINT, V, V), (V * BLOCKS * PD) ** -0.5, 0.0625, ((0, 16),))
    return dict(amps=amps, driver=driver, pattern=pattern, domain=domain, virt_energy=virt_energy, pair_gap=pair_gap, integrals=integrals)


def reference(amps, driver, pattern, domain, virt_energy, pair_gap, integrals):
    width = amps.shape[-1]
    nblk = amps.shape[0]
    rows = jnp.arange(width, dtype=jnp.int32)
    edge = (rows < domain[..., None]).astype(jnp.float32)
    mask = edge[..., :, None] * edge[..., None, :]
    held = amps.astype(jnp.float32) * mask
    tiles_all = integrals.astype(jnp.float32)

    def one_block(index):
        links = pattern[index]

        def step(total, source):
            visit = held[source]
            idx = links[:, :, source, :]
            valid = (idx >= 0).astype(jnp.float32)
            tiles = tiles_all[jnp.maximum(idx, 0)] * valid[..., None, None]
            add = jnp.einsum('gqab,gpqbc->gpac', visit, tiles, precision=lax.Precision.HIGHEST)
            return (total + add, None)
        start = jnp.zeros(held.shape[1:], jnp.float32)
        total, _ = lax.scan(step, start, jnp.arange(nblk, dtype=jnp.int32))
        return total
    coupled = lax.map(one_block, jnp.arange(nblk, dtype=jnp.int32))
    resid = mask * (driver + coupled)
    denom = virt_energy[..., :, None] + virt_energy[..., None, :] + pair_gap[..., None, None]
    new_amps = held + resid / denom
    resid_rms = jnp.sqrt(jnp.sum(resid * resid) / float(resid.size))
    return (new_amps, resid_rms)
```

```python
import functools

import jax
import jax.numpy as jnp
from jax import lax
from jax.experimental import pallas as pl
from jax.experimental.pallas import tpu as pltpu
from jax.sharding import PartitionSpec as P

MESH = pl.DeviceIdType.MESH
NY = 4
NL = 2
NC = 2
PEERS = 8


def far_first(n):
    return sorted(range(1, n), key=lambda d: -min(d, n - d))


def near_first(n):
    return sorted(range(1, n), key=lambda d: min(d, n - d))


def kernel(
    nz,
    nx,
    domain,
    pattern,
    amps,
    driver,
    integrals,
    resid_out,
    total_out,
    amps_v,
    held,
    driver_v,
    table,
    h,
    ints,
    idx,
    drv,
    y_a,
    y_b,
    acc,
    back,
    home,
    parts,
    local_sem,
    z_send,
    z_recv,
    y_send,
    y_recv,
    t_send,
    t_recv,
    r_send,
    r_recv,
    m_send,
    m_recv,
):
    f32 = jnp.float32
    width = held.shape[-1]
    rows = width // nz
    nk = table.shape[0] * 2
    blk = lax.axis_index("blk")
    col = lax.axis_index("col")
    z, yh = blk // NY, blk % NY
    x, yl, core = col // (NL * NC), (col // NC) % NL, col % NC

    def at_z(d):
        return (((z + d) % nz) * NY + yh, col)

    def at_yh(d):
        return (z * NY + (yh + d) % NY, col)

    def at_y(d):
        place = (yh * NL + yl + d) % (NY * NL)
        return (z * NY + place // NL, (x * NL + place % NL) * NC + core)

    def at_xc(d):
        place = (x * NC + core + d) % (nx * NC)
        return (blk, ((place // NC) * NL + yl) * NC + place % NC)

    def at_x(d):
        return (blk, (((x + d) % nx) * NL + yl) * NC + core)

    over = (blk, (x * NL + 1 - yl) * NC + core)
    sibling = (blk, (x * NL + yl) * NC + 1 - core)

    barrier = pltpu.get_barrier_semaphore()
    groups = ((at_z, nz), (at_y, NY * NL), (at_xc, nx * NC))
    for where_to, n in groups:
        for d in far_first(n):
            pl.semaphore_signal(barrier, inc=1, device_id=where_to(d), device_id_type=MESH)

    get_amps = pltpu.make_async_copy(amps, amps_v, local_sem.at[0])
    get_amps.start()
    get_tiles = []
    for j in range(2):
        get = pltpu.make_async_copy(
            integrals.at[j], table.at[col, :, pl.ds(j * width, width)], local_sem.at[1 + j]
        )
        get.start()
        get_tiles.append(get)
    get_driver = pltpu.make_async_copy(driver, driver_v, local_sem.at[3])
    get_driver.start()

    ints[z] = jnp.zeros(ints.shape[1:], jnp.int32)
    lane = lax.broadcasted_iota(jnp.int32, (pattern.shape[1], width), 1)
    sub = lax.broadcasted_iota(jnp.int32, (pattern.shape[1], width), 0)
    for p in range(2):
        both = jnp.where(
            lane % 2 == 0,
            jnp.broadcast_to(pattern[p, :, 0:1], lane.shape),
            jnp.broadcast_to(pattern[p, :, 1:2], lane.shape),
        )
        both = jnp.where(both < 0, nk, both)
        row = jnp.sum(jnp.where(sub == lane // 2, both, 0), axis=0, keepdims=True)
        ints[z, p : p + 1, :] = row
        ints[z, 2 + p : 3 + p, :] = jnp.full((1, width), domain[0, 0, p], jnp.int32)

    get_amps.wait()
    across = lax.broadcasted_iota(jnp.int32, (width, width), 1)
    down = lax.broadcasted_iota(jnp.int32, (width, width), 0)
    for q in range(2):
        inside = (across < domain[0, 0, q]) & (down < domain[0, 0, q])
        held[q] = jnp.where(inside, amps_v[q].astype(f32), 0.0).astype(jnp.bfloat16)
    mine = pl.ds(pl.multiple_of(z * rows, rows), rows)
    for q in range(2):
        h[0, z, q] = held[q, mine, :]
    for get in get_tiles:
        get.wait()
    pl.semaphore_wait(barrier, sum(n - 1 for _, n in groups))

    sends = []

    def send(src, dst, ssem, rsem, where_to):
        copy = pltpu.make_async_remote_copy(
            src_ref=src, dst_ref=dst, send_sem=ssem, recv_sem=rsem,
            device_id=where_to, device_id_type=MESH,
        )
        copy.start()
        sends.append(copy)

    def arrived(ref, ssem, rsem):
        pltpu.make_async_remote_copy(
            src_ref=ref, dst_ref=ref, send_sem=ssem, recv_sem=rsem,
            device_id=sibling, device_id_type=MESH,
        ).wait_recv()

    def their_rows(d):
        return pl.ds(pl.multiple_of(((z + d) % nz) * rows, rows), rows)

    for d in far_first(nz):
        send(held.at[:, their_rows(d), :], h.at[0, z], z_send.at[0, d], z_recv.at[0, d], at_z(d))

    def piece_out(d):
        zz = (z - d + nz) % nz
        send(h.at[0, zz], h.at[1, zz], y_send.at[0, d], y_recv.at[0, d], at_yh(1))
        send(h.at[0, zz], h.at[3, zz], y_send.at[1, d], y_recv.at[1, d], at_yh(NY - 1))

    def piece_from_z(d):
        zz = (z - d + nz) % nz
        arrived(h.at[0, zz], z_send.at[0, d], z_recv.at[0, d])
        piece_out(d)

    def piece_relay(d):
        zz = (z - d + nz) % nz
        arrived(h.at[1, zz], y_send.at[0, d], y_recv.at[0, d])
        send(h.at[1, zz, 0], h.at[2, zz, 0], y_send.at[2, d], y_recv.at[2, d], at_yh(1))
        arrived(h.at[3, zz], y_send.at[1, d], y_recv.at[1, d])
        send(h.at[3, zz, 1], h.at[2, zz, 1], y_send.at[3, d], y_recv.at[3, d], at_yh(NY - 1))

    def unit(dx, other):
        lo = 1 - yl if other else yl
        return table.at[(((x - dx + nx) % nx) * NL + lo) * NC + core]

    def unit_of_sibling(dx, other):
        lo = 1 - yl if other else yl
        return table.at[(((x - dx + nx) % nx) * NL + lo) * NC + 1 - core]

    half = width // 2
    def unit_along_x(other):
        base = 4 if other else 0
        send(unit(0, other), unit(0, other), t_send.at[base], t_recv.at[base], at_x(1))
        send(unit(0, other), unit(0, other), t_send.at[base + 1], t_recv.at[base + 1], at_x(nx - 1))

    def to_sibling(ref, n):
        send(ref, ref, t_send.at[n], t_recv.at[n], sibling)

    def unit_near(other):
        base = 4 if other else 0
        side = 15 if other else 10
        up, down_ = unit(1, other), unit(nx - 1, other)
        arrived(up, t_send.at[base], t_recv.at[base])
        first = up.at[pl.ds(0, half), :]
        send(first, first, t_send.at[base + 2], t_recv.at[base + 2], at_x(1))
        arrived(down_, t_send.at[base + 1], t_recv.at[base + 1])
        second = down_.at[pl.ds(half, half), :]
        send(second, second, t_send.at[base + 3], t_recv.at[base + 3], at_x(nx - 1))
        to_sibling(up, side)
        to_sibling(down_, side + 1)

    def unit_far(other):
        base = 4 if other else 0
        side = 17 if other else 12
        far = unit(2, other)
        for i in range(2):
            part = far.at[pl.ds(i * half, half), :]
            arrived(part, t_send.at[base + 2 + i], t_recv.at[base + 2 + i])
            to_sibling(part, side + i)

    piece_out(0)
    unit_along_x(False)
    send(unit(0, False), unit(0, False), t_send.at[8], t_recv.at[8], over)
    to_sibling(unit(0, False), 9)
    for d in far_first(nz):
        send(ints.at[z], ints.at[z], z_send.at[1, d], z_recv.at[1, d], at_z(d))
    get_driver.wait()
    for d in far_first(nz):
        send(driver_v.at[:, their_rows(d), :], drv.at[z], z_send.at[2, d], z_recv.at[2, d], at_z(d))
    for p in range(2):
        drv[z, p] = driver_v[p, mine, :]

    order = near_first(nz)
    for d in order[:4]:
        piece_from_z(d)
    piece_relay(0)
    unit_near(False)
    arrived(unit(0, True), t_send.at[8], t_recv.at[8])
    unit_along_x(True)
    to_sibling(unit(0, True), 14)
    for d in order[4:6]:
        piece_from_z(d)
    for d in order[:2]:
        piece_relay(d)
    for d in order[6:]:
        piece_from_z(d)
    for d in order[2:4]:
        piece_relay(d)
    unit_far(False)
    for d in order[4:6]:
        piece_relay(d)
    unit_near(True)
    for d in order[6:]:
        piece_relay(d)

    for d in order:
        arrived(ints.at[(z - d + nz) % nz], z_send.at[1, d], z_recv.at[1, d])
    get_idx = pltpu.make_async_copy(ints, idx, local_sem.at[4])
    get_idx.start()
    acc[...] = jnp.zeros_like(acc)
    y_a[nk] = jnp.zeros(y_a.shape[1:], f32)
    y_b[nk] = jnp.zeros(y_b.shape[1:], f32)
    unit_far(True)

    arrived(unit_of_sibling(0, False), t_send.at[9], t_recv.at[9])
    arrived(unit_of_sibling(0, True), t_send.at[14], t_recv.at[14])
    for other in (False, True):
        side = 15 if other else 10
        arrived(unit_of_sibling(1, other), t_send.at[side], t_recv.at[side])
        arrived(unit_of_sibling(nx - 1, other), t_send.at[side + 1], t_recv.at[side + 1])
        far = unit_of_sibling(2, other)
        for i in range(2):
            arrived(far.at[pl.ds(i * half, half), :], t_send.at[side + 2 + i], t_recv.at[side + 2 + i])
    get_idx.wait()

    def couple(dy, y):
        lhs = h[dy].reshape(nz * 2 * rows, width)
        for o in range(table.shape[0]):
            both = jnp.dot(lhs, table[o], preferred_element_type=f32)
            y[2 * o] = both[:, :width].reshape(nz * 2, rows, width)
            y[2 * o + 1] = both[:, width:].reshape(nz * 2, rows, width)
        behind = ((yh - dy + NY) % NY) * 2

        def add_up(g, carry):
            zo, p = g // 2, g % 2
            total = acc[g]
            for zs in range(nz):
                for q in range(2):
                    k = idx[zo, p, zs * NY * 2 + behind + q]
                    total = total + y[k, zs * 2 + q]
            acc[g] = total
            return carry

        lax.fori_loop(0, nz * 2, add_up, 0)

    couple(0, y_a)
    couple(1, y_b)
    couple(3, y_a)
    for d in range(nz):
        zz = (z - d + nz) % nz
        for i in range(2):
            arrived(h.at[2, zz, i], y_send.at[2 + i, d], y_recv.at[2 + i, d])
    couple(2, y_b)

    for d in order:
        arrived(drv.at[(z - d + nz) % nz], z_send.at[2, d], z_recv.at[2, d])
    below = lax.broadcasted_iota(jnp.int32, (rows, width), 0) + z * rows
    aside = lax.broadcasted_iota(jnp.int32, (rows, width), 1)
    squares = jnp.zeros((rows, width), f32)
    for zo in range(nz):
        for p in range(2):
            limit = idx[zo, 2 + p, 0]
            inside = (below < limit) & (aside < limit)
            value = jnp.where(inside, drv[zo, p] + acc[zo * 2 + p], 0.0)
            back[zo, p] = value
            squares = squares + value * value
    squares = jnp.sum(squares.reshape(rows // 8, 8, width), axis=0)

    def stage_out(i, place, where_to, n, value):
        parts[i, place] = value
        for d in far_first(n):
            send(parts.at[i, place], parts.at[i, place], m_send.at[i, d], m_recv.at[i, d], where_to(d))

    def stage_in(i, place, n):
        for d in near_first(n):
            arrived(parts.at[i, (place - d + n) % n], m_send.at[i, d], m_recv.at[i, d])
        total = parts[i, 0]
        for j in range(1, n):
            total = total + parts[i, j]
        return total

    xc, yy = x * NC + core, yh * NL + yl
    stage_out(0, xc, at_xc, nx * NC, squares)
    for d in far_first(nz):
        send(back.at[(z + d) % nz], home.at[:, mine, :], r_send.at[d], r_recv.at[d], at_z(d))
    for p in range(2):
        home[p, mine, :] = back[z, p]
    total = stage_in(0, xc, nx * NC)
    stage_out(1, yy, at_y, NY * NL, total)
    total = stage_in(1, yy, NY * NL)
    stage_out(2, z, at_z, nz, total)
    for d in order:
        theirs = pl.ds(pl.multiple_of(((z - d + nz) % nz) * rows, rows), rows)
        arrived(home.at[:, theirs, :], r_send.at[d], r_recv.at[d])
    resid_out[...] = home[...]
    total = stage_in(2, z, nz)
    total_out[...] = jnp.full(total_out.shape, jnp.sum(total), f32)
    for copy in sends:
        copy.wait_send()


def per_device(amps, driver, pattern, domain, virt_energy, pair_gap, integrals):
    width = amps.shape[-1]
    per_block = amps.shape[2]
    nz = lax.axis_size("blk") // NY
    nx = lax.axis_size("col") // (NL * NC)
    rows_of = width // nz
    owners = lax.axis_size("col")
    nk = owners * integrals.shape[0]
    dma = pltpu.SemaphoreType.DMA
    anywhere = pl.BlockSpec(memory_space=pl.ANY)
    in_vmem = pl.BlockSpec(memory_space=pltpu.VMEM)
    tile = (width, width)
    resid, total = pl.pallas_call(
        functools.partial(kernel, nz, nx),
        out_shape=(
            jax.ShapeDtypeStruct((per_block, *tile), jnp.float32),
            jax.ShapeDtypeStruct((8, width), jnp.float32),
        ),
        in_specs=[pl.BlockSpec(memory_space=pltpu.SMEM), in_vmem, anywhere, anywhere, anywhere],
        out_specs=(in_vmem, in_vmem),
        scratch_shapes=[
            pltpu.VMEM((2, *tile), jnp.bfloat16),
            pltpu.VMEM((2, *tile), jnp.bfloat16),
            pltpu.VMEM((2, *tile), jnp.float32),
            pltpu.VMEM((owners, width, 2 * width), jnp.bfloat16),
            pltpu.VMEM((NY, nz, 2, rows_of, width), jnp.bfloat16),
            pltpu.VMEM((nz, 8, width), jnp.int32),
            pltpu.SMEM((nz, 8, width), jnp.int32),
            pltpu.VMEM((nz, 2, rows_of, width), jnp.float32),
            pltpu.VMEM((nk + 1, nz * 2, rows_of, width), jnp.float32),
            pltpu.VMEM((nk + 1, nz * 2, rows_of, width), jnp.float32),
            pltpu.VMEM((nz * 2, rows_of, width), jnp.float32),
            pltpu.VMEM((nz, 2, rows_of, width), jnp.float32),
            pltpu.VMEM((2, *tile), jnp.float32),
            pltpu.VMEM((3, PEERS, 8, width), jnp.float32),
            dma((5,)),
            dma((3, nz)),
            dma((3, nz)),
            dma((4, nz)),
            dma((4, nz)),
            dma((19,)),
            dma((19,)),
            dma((nz,)),
            dma((nz,)),
            dma((3, PEERS)),
            dma((3, PEERS)),
        ],
        compiler_params=pltpu.CompilerParams(
            collective_id=0, has_side_effects=True, vmem_limit_bytes=32 * 1024 * 1024
        ),
    )(domain, pattern[0, 0], amps[0, 0], driver[0, 0], integrals)

    rows = jnp.arange(width, dtype=jnp.int32)
    edge = rows[None, :] < domain[0, 0][:, None]
    inside = edge[:, :, None] & edge[:, None, :]
    energy = virt_energy[0, 0]
    denom = energy[:, :, None] + energy[:, None, :] + pair_gap[0, 0][:, None, None]
    held = jnp.where(inside, amps[0, 0].astype(jnp.float32), 0.0)
    new_amps = held + resid / denom
    entries = float(lax.axis_size("blk") * owners * per_block * width * width)
    resid_rms = jnp.sqrt(total[0, 0] / entries)
    return (new_amps[None, None], resid_rms)


def solution(mesh):
    in_specs = (
        P("blk", "col", None, None, None),
        P("blk", "col", None, None, None),
        P("blk", "col", None, None, None),
        P("blk", "col", None),
        P("blk", "col", None, None),
        P("blk", "col", None),
        P("col", None, None),
    )
    out_specs = (P("blk", "col", None, None, None), P())
    return jax.shard_map(
        per_device, mesh=mesh, in_specs=in_specs, out_specs=out_specs, check_vma=False
    )
```

```python
import functools

import jax
import jax.numpy as jnp
from jax import lax
from jax.experimental import pallas as pl
from jax.experimental.pallas import tpu as pltpu
from jax.sharding import PartitionSpec as P

MESH = pl.DeviceIdType.MESH
NY = 4
NL = 2
NC = 2


def far_first(n):
    return sorted(range(1, n), key=lambda d: -min(d, n - d))


def near_first(n):
    return sorted(range(1, n), key=lambda d: min(d, n - d))


def kernel(
    nz,
    nx,
    entries,
    domain,
    pattern,
    amps,
    driver,
    energy,
    gap,
    integrals,
    amps_out,
    rms_out,
    domain_s,
    gap_s,
    pattern_v,
    energy_v,
    amps_v,
    held,
    driver_v,
    denom,
    table,
    h,
    ints,
    idx,
    drv,
    y_near,
    y_far,
    acc,
    back,
    home,
    parts,
    local_sem,
    z_send,
    z_recv,
    y_send,
    y_recv,
    t_send,
    t_recv,
    r_send,
    r_recv,
    m_send,
    m_recv,
):
    f32 = jnp.float32
    width = held.shape[-1]
    rows = width // nz
    nk = table.shape[0] * 2
    blk = lax.axis_index("blk")
    col = lax.axis_index("col")
    z, yh = blk // NY, blk % NY
    x, yl, core = col // (NL * NC), (col // NC) % NL, col % NC

    def at_z(d):
        return (((z + d) % nz) * NY + yh, col)

    def at_yh(d):
        return (z * NY + (yh + d) % NY, col)

    def at_y(d):
        place = (yh * NL + yl + d) % (NY * NL)
        return (z * NY + place // NL, (x * NL + place % NL) * NC + core)

    def at_x(d):
        return (blk, (((x + d) % nx) * NL + yl) * NC + core)

    def at_zc(d, e):
        return (((z + d) % nz) * NY + yh, (x * NL + yl) * NC + (core + e) % NC)

    over = (blk, (x * NL + 1 - yl) * NC + core)
    sibling = (blk, (x * NL + yl) * NC + 1 - core)
    zc_far = [(d, e) for d in far_first(nz) for e in range(NC)] + [(0, 1)]

    barrier = pltpu.get_barrier_semaphore()
    greeted = [at_zc(d, e) for d, e in zc_far]
    greeted += [at_y(d) for d in far_first(NY * NL)]
    greeted += [at_x(d) for d in far_first(nx)]
    for device in greeted:
        pl.semaphore_signal(barrier, inc=1, device_id=device, device_id_type=MESH)

    gets = []
    for src, dst in (
        (domain, domain_s),
        (amps, amps_v),
        (pattern, pattern_v),
        (integrals.at[0], table.at[col, :, pl.ds(0, width)]),
        (integrals.at[1], table.at[col, :, pl.ds(width, width)]),
        (driver, driver_v),
        (energy, energy_v),
        (gap, gap_s),
    ):
        get = pltpu.make_async_copy(src, dst, local_sem.at[len(gets)])
        get.start()
        gets.append(get)

    across = lax.broadcasted_iota(jnp.int32, (width, width), 1)
    down = lax.broadcasted_iota(jnp.int32, (width, width), 0)
    mine = pl.ds(pl.multiple_of(z * rows, rows), rows)
    gets[0].wait()
    gets[1].wait()
    for q in range(2):
        inside = (across < domain_s[0, 0, q]) & (down < domain_s[0, 0, q])
        held[q] = jnp.where(inside, amps_v[q].astype(f32), 0.0).astype(jnp.bfloat16)
    for q in range(2):
        h[0, 0, q] = held[q, mine, :]

    gets[2].wait()
    ints[z] = jnp.zeros(ints.shape[1:], jnp.int32)
    places = pattern_v.shape[-1]
    for p in range(2):
        tiles = pattern_v[p]
        ints[z, 2 * p : 2 * p + 2, 0:places] = jnp.where(tiles < 0, nk, tiles)
        ints[z, 4 + p : 5 + p, :] = jnp.full((1, width), domain_s[0, 0, p], jnp.int32)

    gets[3].wait()
    gets[4].wait()
    pl.semaphore_wait(barrier, len(greeted))

    sends = []

    def send(src, dst, ssem, rsem, where_to):
        copy = pltpu.make_async_remote_copy(
            src_ref=src, dst_ref=dst, send_sem=ssem, recv_sem=rsem,
            device_id=where_to, device_id_type=MESH,
        )
        copy.start()
        sends.append(copy)

    def arrived(ref, ssem, rsem):
        pltpu.make_async_remote_copy(
            src_ref=ref, dst_ref=ref, send_sem=ssem, recv_sem=rsem,
            device_id=sibling, device_id_type=MESH,
        ).wait_recv()

    def their_rows(d):
        return pl.ds(pl.multiple_of(((z + d) % nz) * rows, rows), rows)

    order = near_first(nz)
    slot = {d: i for i, d in enumerate([0] + order)}

    for d in far_first(nz):
        send(held.at[:, their_rows(d), :], h.at[slot[d], 0], z_send.at[0, d], z_recv.at[0, d], at_z(d))

    def piece_out(d):
        piece = h.at[slot[d], 0]
        for dy in (2, 1, 3):
            send(piece, h.at[slot[d], dy], y_send.at[d, dy], y_recv.at[d, dy], at_yh(dy))

    def piece_from_z(d):
        arrived(h.at[slot[d], 0], z_send.at[0, d], z_recv.at[0, d])
        piece_out(d)

    def owner(dx, other, far_core):
        lo = 1 - yl if other else yl
        return (((x - dx + nx) % nx) * NL + lo) * NC + (1 - core if far_core else core)

    def unit(dx, other, far_core=0):
        return table.at[owner(dx, other, far_core)]

    def kind(dx, other, far_core=0):
        return dx + nx * other + 2 * nx * far_core

    def unit_along_x(other):
        n = unit(0, other)
        for d in far_first(nx):
            send(n, n, t_send.at[kind(d, other)], t_recv.at[kind(d, other)], at_x(d))

    def unit_to_sibling(dx, other):
        n = unit(dx, other)
        send(n, n, t_send.at[kind(dx, other, 1)], t_recv.at[kind(dx, other, 1)], sibling)

    def unit_in(dx, other, far_core=0):
        n = kind(dx, other, far_core)
        arrived(unit(dx, other, far_core), t_send.at[n], t_recv.at[n])

    def unit_from_x(dx, other):
        unit_in(dx, other)
        unit_to_sibling(dx, other)

    send(unit(0, 0), unit(0, 0), t_send.at[kind(0, 1)], t_recv.at[kind(0, 1)], over)
    unit_along_x(0)
    piece_out(0)
    unit_to_sibling(0, 0)
    for d in far_first(nz):
        send(ints.at[z], ints.at[z], z_send.at[1, d], z_recv.at[1, d], at_z(d))
    gets[5].wait()
    for d in far_first(nz):
        send(driver_v.at[:, their_rows(d), :], drv.at[z], z_send.at[2, d], z_recv.at[2, d], at_z(d))
    for p in range(2):
        drv[z, p] = driver_v[p, mine, :]
    acc[...] = jnp.zeros_like(acc)
    y_near[nk] = jnp.zeros(y_near.shape[1:], f32)
    y_far[nk] = jnp.zeros(y_far.shape[1:], f32)

    for d in order[:4]:
        piece_from_z(d)
    unit_in(0, 1)
    unit_along_x(1)
    unit_to_sibling(0, 1)
    for d in order[4:6]:
        piece_from_z(d)
    for d in near_first(nx)[:2]:
        unit_from_x(d, 0)
    for d in order[6:]:
        piece_from_z(d)
    for d in near_first(nx)[2:]:
        unit_from_x(d, 0)

    for d in order:
        arrived(ints.at[(z - d + nz) % nz], z_send.at[1, d], z_recv.at[1, d])
    get_idx = pltpu.make_async_copy(ints, idx, local_sem.at[len(gets)])
    get_idx.start()
    gets[6].wait()
    gets[7].wait()
    for p in range(2):
        own = jnp.broadcast_to(energy_v[0, 0, p : p + 1, :], (width, width))
        turned = jnp.sum(jnp.where(across == down, own, 0.0), axis=1, keepdims=True)
        denom[p] = turned + own + gap_s[0, 0, p]
    for d in near_first(nx):
        unit_from_x(d, 1)
    get_idx.wait()

    def pieces_in(ds):
        for d in ds:
            for dy in (1, 3, 2):
                arrived(h.at[slot[d], dy], y_send.at[d, dy], y_recv.at[d, dy])

    def couple(ds, y, wait_units):
        first, count = slot[ds[0]], len(ds)
        lhs = h[first : first + count].reshape(count * NY * 2 * rows, width)
        for far_core in range(2):
            for other in range(2):
                for dx in [0] + near_first(nx):
                    if wait_units and far_core:
                        unit_in(dx, other, 1)
                    o = owner(dx, other, far_core)
                    both = jnp.dot(lhs, table[o], preferred_element_type=f32)
                    y[2 * o] = both[:, :width].reshape(count * NY * 2, rows, width)
                    y[2 * o + 1] = both[:, width:].reshape(count * NY * 2, rows, width)
        behind = [[((z - d + nz) % nz) * NY + (yh - dy + NY) % NY for dy in range(NY)] for d in ds]

        def add_up(g, carry):
            zo, p = g // 2, g % 2
            total = acc[g]
            for i in range(count):
                for dy in range(NY):
                    for q in range(2):
                        k = idx[zo, p * 2 + q, behind[i][dy]]
                        total = total + y[k, (i * NY + dy) * 2 + q]
            acc[g] = total
            return carry

        lax.fori_loop(0, nz * 2, add_up, 0)

    near = [0] + order[:4]
    pieces_in(near)
    couple(near, y_near, True)
    pieces_in(order[4:])
    couple(order[4:], y_far, False)

    for d in order:
        arrived(drv.at[(z - d + nz) % nz], z_send.at[2, d], z_recv.at[2, d])
    below = lax.broadcasted_iota(jnp.int32, (rows, width), 0) + z * rows
    aside = lax.broadcasted_iota(jnp.int32, (rows, width), 1)
    squares = jnp.zeros((rows, width), f32)
    for zo in range(nz):
        for p in range(2):
            limit = idx[zo, 4 + p, 0]
            inside = (below < limit) & (aside < limit)
            value = jnp.where(inside, drv[zo, p] + acc[zo * 2 + p], 0.0)
            back[zo, p] = value
            squares = squares + value * value
    squares = jnp.sum(squares, axis=0, keepdims=True)

    def stage_out(i, place, peers, value):
        parts[i, place] = value
        for j, device in enumerate(peers):
            send(parts.at[i, place], parts.at[i, place], m_send.at[i, j], m_recv.at[i, j], device)

    def stage_in(i, places):
        for j, place in reversed(list(enumerate(places))):
            arrived(parts.at[i, place], m_send.at[i, j], m_recv.at[i, j])
        total = parts[i, 0]
        for j in range(1, len(places) + 1):
            total = total + parts[i, j]
        return total

    yy, ny = yh * NL + yl, NY * NL
    stage_out(0, z * NC + core, [at_zc(d, e) for d, e in zc_far], squares)
    for d in far_first(nz):
        send(back.at[(z + d) % nz], home.at[:, mine, :], r_send.at[d], r_recv.at[d], at_z(d))
    for p in range(2):
        home[p, mine, :] = back[z, p]
    total = stage_in(0, [((z - d + nz) % nz) * NC + (core + e) % NC for d, e in zc_far])
    stage_out(1, yy, [at_y(d) for d in far_first(ny)], total)
    total = stage_in(1, [(yy - d + ny) % ny for d in far_first(ny)])
    stage_out(2, x, [at_x(d) for d in far_first(nx)], total)
    for d in order:
        theirs = pl.ds(pl.multiple_of(((z - d + nz) % nz) * rows, rows), rows)
        arrived(home.at[:, theirs, :], r_send.at[d], r_recv.at[d])
    for p in range(2):
        amps_out[p] = held[p].astype(f32) + home[p] / denom[p]
    total = stage_in(2, [(x - d + nx) % nx for d in far_first(nx)])
    rms_out[0, 0] = jnp.max(jnp.sqrt(jnp.full((8, width), jnp.sum(total) / entries, f32)))
    for copy in sends:
        copy.wait_send()


def per_device(amps, driver, pattern, domain, virt_energy, pair_gap, integrals):
    width = amps.shape[-1]
    per_block = amps.shape[2]
    nz = lax.axis_size("blk") // NY
    nx = lax.axis_size("col") // (NL * NC)
    rows_of = width // nz
    owners = lax.axis_size("col")
    nk = owners * integrals.shape[0]
    entries = float(lax.axis_size("blk") * owners * per_block * width * width)
    near = 5
    dma = pltpu.SemaphoreType.DMA
    in_hbm = pl.BlockSpec(memory_space=pltpu.HBM)
    tile = (width, width)
    new_amps, rms = pl.pallas_call(
        functools.partial(kernel, nz, nx, entries),
        out_shape=(
            jax.ShapeDtypeStruct((per_block, *tile), jnp.float32),
            jax.ShapeDtypeStruct((1, 1), jnp.float32),
        ),
        in_specs=[in_hbm] * 7,
        out_specs=(pl.BlockSpec(memory_space=pltpu.VMEM), pl.BlockSpec(memory_space=pltpu.SMEM)),
        scratch_shapes=[
            pltpu.SMEM((1, 1, 2), jnp.int32),
            pltpu.SMEM((1, 1, 2), jnp.float32),
            pltpu.VMEM((2, 2, pattern.shape[3]), jnp.int32),
            pltpu.VMEM((1, 1, 2, width), jnp.float32),
            pltpu.VMEM((2, *tile), jnp.bfloat16),
            pltpu.VMEM((2, *tile), jnp.bfloat16),
            pltpu.VMEM((2, *tile), jnp.float32),
            pltpu.VMEM((2, *tile), jnp.float32),
            pltpu.VMEM((owners, width, 2 * width), jnp.bfloat16),
            pltpu.VMEM((nz, NY, 2, rows_of, width), jnp.bfloat16),
            pltpu.VMEM((nz, 8, width), jnp.int32),
            pltpu.SMEM((nz, 8, width), jnp.int32),
            pltpu.VMEM((nz, 2, rows_of, width), jnp.float32),
            pltpu.VMEM((nk + 1, near * NY * 2, rows_of, width), jnp.float32),
            pltpu.VMEM((nk + 1, (nz - near) * NY * 2, rows_of, width), jnp.float32),
            pltpu.VMEM((nz * 2, rows_of, width), jnp.float32),
            pltpu.VMEM((nz, 2, rows_of, width), jnp.float32),
            pltpu.VMEM((2, *tile), jnp.float32),
            pltpu.VMEM((3, nz * NC, 1, width), jnp.float32),
            dma((9,)),
            dma((3, nz)),
            dma((3, nz)),
            dma((nz, NY)),
            dma((nz, NY)),
            dma((4 * nx,)),
            dma((4 * nx,)),
            dma((nz,)),
            dma((nz,)),
            dma((3, nz * NC)),
            dma((3, nz * NC)),
        ],
        compiler_params=pltpu.CompilerParams(
            collective_id=0, has_side_effects=True, vmem_limit_bytes=67043328
        ),
    )(
        domain,
        jnp.swapaxes(pattern[0, 0], 1, 2),
        amps[0, 0],
        driver[0, 0],
        virt_energy,
        pair_gap,
        integrals,
    )
    return (new_amps[None, None], rms.reshape(()))


def solution(mesh):
    in_specs = (
        P("blk", "col", None, None, None),
        P("blk", "col", None, None, None),
        P("blk", "col", None, None, None),
        P("blk", "col", None),
        P("blk", "col", None, None),
        P("blk", "col", None),
        P("col", None, None),
    )
    out_specs = (P("blk", "col", None, None, None), P())
    return jax.shard_map(
        per_device, mesh=mesh, in_specs=in_specs, out_specs=out_specs, check_vma=False
    )
```

```python
import functools

import jax
import jax.numpy as jnp
from jax import lax
from jax.experimental import pallas as pl
from jax.experimental.pallas import tpu as pltpu
from jax.sharding import PartitionSpec as P

MESH = pl.DeviceIdType.MESH
NY = 4
NL = 2
NC = 2


def far_first(n):
    return sorted(range(1, n), key=lambda d: -min(d, n - d))


def near_first(n):
    return sorted(range(1, n), key=lambda d: min(d, n - d))


def kernel(
    nz,
    nx,
    entries,
    domain,
    pattern,
    amps,
    driver,
    energy,
    gap,
    integrals,
    amps_out,
    rms_out,
    domain_s,
    gap_s,
    pattern_v,
    energy_v,
    amps_v,
    held,
    driver_v,
    denom,
    table,
    h_own,
    h_near,
    h_far,
    lanes,
    ints_out,
    ints,
    idx,
    drv,
    y_own,
    y_near,
    y_far,
    acc,
    back,
    home,
    parts,
    local_sem,
    z_send,
    z_recv,
    y_send,
    y_recv,
    t_send,
    t_recv,
    r_send,
    r_recv,
    m_send,
    m_recv,
):
    f32 = jnp.float32
    width = held.shape[-1]
    rows = width // nz
    nk = table.shape[0] * 2
    blk = lax.axis_index("blk")
    col = lax.axis_index("col")
    z, yh = blk // NY, blk % NY
    x, yl, core = col // (NL * NC), (col // NC) % NL, col % NC

    def at_z(d):
        return (((z + d) % nz) * NY + yh, col)

    def at_yh(d):
        return (z * NY + (yh + d) % NY, col)

    def at_y(d):
        place = (yh * NL + yl + d) % (NY * NL)
        return (z * NY + place // NL, (x * NL + place % NL) * NC + core)

    def at_x(d):
        return (blk, (((x + d) % nx) * NL + yl) * NC + core)

    def at_zc(d, e):
        return (((z + d) % nz) * NY + yh, (x * NL + yl) * NC + (core + e) % NC)

    over = (blk, (x * NL + 1 - yl) * NC + core)
    sibling = (blk, (x * NL + yl) * NC + 1 - core)
    zc_far = [(d, e) for d in far_first(nz) for e in range(NC)] + [(0, 1)]

    barrier = pltpu.get_barrier_semaphore()
    greeted = [at_zc(d, e) for d, e in zc_far]
    greeted += [at_y(d) for d in far_first(NY * NL)]
    greeted += [at_x(d) for d in far_first(nx)]
    for device in greeted:
        pl.semaphore_signal(barrier, inc=1, device_id=device, device_id_type=MESH)

    gets = []
    for src, dst in (
        (domain, domain_s),
        (amps, amps_v),
        (pattern, pattern_v),
        (integrals.at[0], table.at[col, :, pl.ds(0, width)]),
        (integrals.at[1], table.at[col, :, pl.ds(width, width)]),
        (driver, driver_v),
        (energy, energy_v),
        (gap, gap_s),
    ):
        get = pltpu.make_async_copy(src, dst, local_sem.at[len(gets)])
        get.start()
        gets.append(get)

    across = lax.broadcasted_iota(jnp.int32, (width, width), 1)
    down = lax.broadcasted_iota(jnp.int32, (width, width), 0)
    mine = pl.ds(pl.multiple_of(z * rows, rows), rows)
    gets[0].wait()
    gets[1].wait()
    for q in range(2):
        inside = (across < domain_s[0, 0, q]) & (down < domain_s[0, 0, q])
        held[q] = jnp.where(inside, amps_v[q].astype(f32), 0.0).astype(jnp.bfloat16)
    for q in range(2):
        h_own[0, q] = held[q, mine, :]

    gets[2].wait()
    lanes[...] = jnp.zeros_like(lanes)
    places = pattern_v.shape[-1]
    for p in range(2):
        tiles = pattern_v[p]
        lanes[2 * p : 2 * p + 2, 0:places] = jnp.where(tiles < 0, nk, tiles)
    spread = lanes[...]
    n = places
    while n < width:
        spread = spread + pltpu.roll(spread, n, 1)
        n *= 2
    lane = lax.broadcasted_iota(jnp.int32, lanes.shape, 1)
    sub = lax.broadcasted_iota(jnp.int32, lanes.shape, 0)
    spread = jnp.where(
        lane % NY + yh < NY,
        pltpu.roll(spread, (width - yh) % width, 1),
        pltpu.roll(spread, (width - yh + NY) % width, 1),
    )
    for d in range(nz):
        turned = pltpu.roll(spread, (width - NY * ((z + d) % nz)) % width, 1)
        turned = jnp.where(sub == 4, domain_s[0, 0, 0], jnp.where(sub == 5, domain_s[0, 0, 1], turned))
        ints_out[d] = turned

    gets[3].wait()
    gets[4].wait()
    pl.semaphore_wait(barrier, len(greeted))

    sends = []

    def send(src, dst, ssem, rsem, where_to):
        copy = pltpu.make_async_remote_copy(
            src_ref=src, dst_ref=dst, send_sem=ssem, recv_sem=rsem,
            device_id=where_to, device_id_type=MESH,
        )
        copy.start()
        sends.append(copy)

    def arrived(ref, ssem, rsem):
        pltpu.make_async_remote_copy(
            src_ref=ref, dst_ref=ref, send_sem=ssem, recv_sem=rsem,
            device_id=sibling, device_id_type=MESH,
        ).wait_recv()

    def their_rows(d):
        return pl.ds(pl.multiple_of(((z + d) % nz) * rows, rows), rows)

    order = near_first(nz)
    slot = {d: i for i, d in enumerate([0] + order)}
    near = h_near.shape[0]

    def piece(d, dy):
        if dy == 0:
            return h_own.at[slot[d]]
        if slot[d] < near:
            return h_near.at[slot[d], dy - 1]
        return h_far.at[slot[d] - near, dy - 1]

    for d in far_first(nz):
        send(held.at[:, their_rows(d), :], piece(d, 0), z_send.at[0, d], z_recv.at[0, d], at_z(d))

    def piece_out(d):
        for dy in (2, 1, 3):
            send(piece(d, 0), piece(d, dy), y_send.at[d, dy], y_recv.at[d, dy], at_yh(dy))

    def piece_from_z(d):
        arrived(piece(d, 0), z_send.at[0, d], z_recv.at[0, d])
        piece_out(d)

    def owner(dx, other, far_core):
        lo = 1 - yl if other else yl
        return (((x - dx + nx) % nx) * NL + lo) * NC + (1 - core if far_core else core)

    def unit(dx, other, far_core=0):
        return table.at[owner(dx, other, far_core)]

    def kind(dx, other, far_core=0):
        return dx + nx * other + 2 * nx * far_core

    def unit_along_x(other):
        n = unit(0, other)
        for d in far_first(nx):
            send(n, n, t_send.at[kind(d, other)], t_recv.at[kind(d, other)], at_x(d))

    def unit_to_sibling(dx, other):
        n = unit(dx, other)
        send(n, n, t_send.at[kind(dx, other, 1)], t_recv.at[kind(dx, other, 1)], sibling)

    def unit_in(dx, other, far_core=0):
        n = kind(dx, other, far_core)
        arrived(unit(dx, other, far_core), t_send.at[n], t_recv.at[n])

    def unit_from_x(dx, other):
        unit_in(dx, other)
        unit_to_sibling(dx, other)

    send(unit(0, 0), unit(0, 0), t_send.at[kind(0, 1)], t_recv.at[kind(0, 1)], over)
    unit_along_x(0)
    piece_out(0)
    unit_to_sibling(0, 0)
    for d in far_first(nz):
        send(ints_out.at[d], ints.at[z], z_send.at[1, d], z_recv.at[1, d], at_z(d))
    gets[5].wait()
    for d in far_first(nz):
        send(driver_v.at[:, their_rows(d), :], drv.at[z], z_send.at[2, d], z_recv.at[2, d], at_z(d))
    for p in range(2):
        drv[z, p] = driver_v[p, mine, :]
    ints[z] = ints_out[0]
    for y in (y_own, y_near, y_far):
        y[:, nk] = jnp.zeros((y.shape[0], *y.shape[2:]), f32)

    for d in order[:4]:
        piece_from_z(d)
    unit_in(0, 1)
    unit_along_x(1)
    unit_to_sibling(0, 1)
    for d in order[4:6]:
        piece_from_z(d)
    for d in near_first(nx)[:2]:
        unit_from_x(d, 0)
    for d in order[6:]:
        piece_from_z(d)
    for d in near_first(nx)[2:]:
        unit_from_x(d, 0)

    for d in order:
        arrived(ints.at[(z - d + nz) % nz], z_send.at[1, d], z_recv.at[1, d])
    get_idx = pltpu.make_async_copy(ints, idx, local_sem.at[len(gets)])
    get_idx.start()
    gets[6].wait()
    gets[7].wait()
    for p in range(2):
        own = jnp.broadcast_to(energy_v[0, 0, p : p + 1, :], (width, width))
        turned = jnp.sum(jnp.where(across == down, own, 0.0), axis=1, keepdims=True)
        denom[p] = turned + own + gap_s[0, 0, p]

    def rows_of(h):
        count = h.size // width
        return h[...].reshape(count, width)

    def products(lhs, y, dx, other, far_core):
        o = owner(dx, other, far_core)
        both = jnp.dot(lhs, table[o], preferred_element_type=f32)
        y[:, 2 * o] = both[:, :width].reshape(y.shape[0], rows, width)
        y[:, 2 * o + 1] = both[:, width:].reshape(y.shape[0], rows, width)

    def add_up(pieces, y, first):
        def step(zo, carry):
            for p in range(2):
                total = None if first else acc[zo * 2 + p]
                for i, (d, dy) in enumerate(pieces):
                    place = ((nz - d) % nz) * NY + (NY - dy) % NY
                    for q in range(2):
                        k = idx[zo, p * 2 + q, place]
                        term = y[i * 2 + q, k]
                        total = term if total is None else total + term
                acc[zo * 2 + p] = total
            return carry

        lax.fori_loop(0, nz, step, 0)

    own_units = [(0, 0), (0, 1)] + [(dx, 0) for dx in near_first(nx)]
    late_units = [(dx, 1) for dx in near_first(nx)]
    lhs = rows_of(h_own)
    for dx, other in own_units:
        products(lhs, y_own, dx, other, 0)
    for dx, other in late_units:
        unit_from_x(dx, other)
    for dx, other in late_units:
        products(lhs, y_own, dx, other, 0)
    units = [(dx, other, 0) for dx, other in own_units + late_units]
    for dx, other in own_units + late_units:
        unit_in(dx, other, 1)
        products(lhs, y_own, dx, other, 1)
        units.append((dx, other, 1))
    get_idx.wait()
    add_up([(d, 0) for d in [0] + order], y_own, True)

    ahead = [0] + order
    for h, y, ds in ((h_near, y_near, ahead[:near]), (h_far, y_far, ahead[near:])):
        pieces = [(d, dy) for d in ds for dy in range(1, NY)]
        for d, dy in pieces:
            arrived(piece(d, dy), y_send.at[d, dy], y_recv.at[d, dy])
        lhs = rows_of(h)
        for n in units:
            products(lhs, y, *n)
        add_up(pieces, y, False)

    for d in order:
        arrived(drv.at[(z - d + nz) % nz], z_send.at[2, d], z_recv.at[2, d])
    below = lax.broadcasted_iota(jnp.int32, (rows, width), 0) + z * rows
    aside = lax.broadcasted_iota(jnp.int32, (rows, width), 1)
    squares = jnp.zeros((rows, width), f32)
    for zo in range(nz):
        for p in range(2):
            limit = idx[zo, 4 + p, 0]
            inside = (below < limit) & (aside < limit)
            value = jnp.where(inside, drv[zo, p] + acc[zo * 2 + p], 0.0)
            back[zo, p] = value
            squares = squares + value * value
    squares = jnp.sum(squares, axis=0, keepdims=True)

    def stage_out(i, place, peers, value):
        parts[i, place] = value
        for j, device in enumerate(peers):
            send(parts.at[i, place], parts.at[i, place], m_send.at[i, j], m_recv.at[i, j], device)

    def stage_in(i, places):
        for j, place in reversed(list(enumerate(places))):
            arrived(parts.at[i, place], m_send.at[i, j], m_recv.at[i, j])
        total = parts[i, 0]
        for j in range(1, len(places) + 1):
            total = total + parts[i, j]
        return total

    yy, ny = yh * NL + yl, NY * NL
    stage_out(0, z * NC + core, [at_zc(d, e) for d, e in zc_far], squares)
    for d in far_first(nz):
        send(back.at[(z + d) % nz], home.at[:, mine, :], r_send.at[d], r_recv.at[d], at_z(d))
    for p in range(2):
        home[p, mine, :] = back[z, p]
    total = stage_in(0, [((z - d + nz) % nz) * NC + (core + e) % NC for d, e in zc_far])
    stage_out(1, yy, [at_y(d) for d in far_first(ny)], total)
    total = stage_in(1, [(yy - d + ny) % ny for d in far_first(ny)])
    stage_out(2, x, [at_x(d) for d in far_first(nx)], total)
    for d in order:
        theirs = pl.ds(pl.multiple_of(((z - d + nz) % nz) * rows, rows), rows)
        arrived(home.at[:, theirs, :], r_send.at[d], r_recv.at[d])
    for p in range(2):
        amps_out[p] = held[p].astype(f32) + home[p] / denom[p]
    for copy in sends:
        copy.wait_send()
    total = stage_in(2, [(x - d + nx) % nx for d in far_first(nx)])
    rms_out[0, 0] = jnp.max(jnp.sqrt(jnp.full((8, width), jnp.sum(total) / entries, f32)))


def per_device(amps, driver, pattern, domain, virt_energy, pair_gap, integrals):
    width = amps.shape[-1]
    per_block = amps.shape[2]
    nz = lax.axis_size("blk") // NY
    nx = lax.axis_size("col") // (NL * NC)
    rows_of = width // nz
    owners = lax.axis_size("col")
    nk = owners * integrals.shape[0]
    entries = float(lax.axis_size("blk") * owners * per_block * width * width)
    near = 5
    dma = pltpu.SemaphoreType.DMA
    in_hbm = pl.BlockSpec(memory_space=pltpu.HBM)
    tile = (width, width)
    operands = (
        domain,
        jnp.swapaxes(pattern[0, 0], 1, 2),
        amps[0, 0],
        driver[0, 0],
        virt_energy,
        pair_gap,
        integrals,
    )
    new_amps, rms = pl.pallas_call(
        functools.partial(kernel, nz, nx, entries),
        out_shape=(
            jax.ShapeDtypeStruct((per_block, *tile), jnp.float32),
            jax.ShapeDtypeStruct((1, 1), jnp.float32),
        ),
        in_specs=[in_hbm] * 7,
        out_specs=(pl.BlockSpec(memory_space=pltpu.VMEM), pl.BlockSpec(memory_space=pltpu.SMEM)),
        scratch_shapes=[
            pltpu.SMEM((1, 1, 2), jnp.int32),
            pltpu.SMEM((1, 1, 2), jnp.float32),
            pltpu.VMEM((2, 2, pattern.shape[3]), jnp.int32),
            pltpu.VMEM((1, 1, 2, width), jnp.float32),
            pltpu.VMEM((2, *tile), jnp.bfloat16),
            pltpu.VMEM((2, *tile), jnp.bfloat16),
            pltpu.VMEM((2, *tile), jnp.float32),
            pltpu.VMEM((2, *tile), jnp.float32),
            pltpu.VMEM((owners, width, 2 * width), jnp.bfloat16),
            pltpu.VMEM((nz, 2, rows_of, width), jnp.bfloat16),
            pltpu.VMEM((near, NY - 1, 2, rows_of, width), jnp.bfloat16),
            pltpu.VMEM((nz - near, NY - 1, 2, rows_of, width), jnp.bfloat16),
            pltpu.VMEM((8, width), jnp.int32),
            pltpu.VMEM((nz, 8, width), jnp.int32),
            pltpu.VMEM((nz, 8, width), jnp.int32),
            pltpu.SMEM((nz, 8, width), jnp.int32),
            pltpu.VMEM((nz, 2, rows_of, width), jnp.float32),
            pltpu.VMEM((nz * 2, nk + 1, rows_of, width), jnp.float32),
            pltpu.VMEM((near * (NY - 1) * 2, nk + 1, rows_of, width), jnp.float32),
            pltpu.VMEM(((nz - near) * (NY - 1) * 2, nk + 1, rows_of, width), jnp.float32),
            pltpu.VMEM((nz * 2, rows_of, width), jnp.float32),
            pltpu.VMEM((nz, 2, rows_of, width), jnp.float32),
            pltpu.VMEM((2, *tile), jnp.float32),
            pltpu.VMEM((3, nz * NC, 1, width), jnp.float32),
            dma((9,)),
            dma((3, nz)),
            dma((3, nz)),
            dma((nz, NY)),
            dma((nz, NY)),
            dma((4 * nx,)),
            dma((4 * nx,)),
            dma((nz,)),
            dma((nz,)),
            dma((3, nz * NC)),
            dma((3, nz * NC)),
        ],
        compiler_params=pltpu.CompilerParams(
            collective_id=0, has_side_effects=True, vmem_limit_bytes=40 * 1024 * 1024
        ),
    )(
        *(pltpu.with_memory_space_constraint(a, pltpu.HBM) for a in operands)
    )
    return (new_amps[None, None], rms.reshape(()))


def solution(mesh):
    in_specs = (
        P("blk", "col", None, None, None),
        P("blk", "col", None, None, None),
        P("blk", "col", None, None, None),
        P("blk", "col", None),
        P("blk", "col", None, None),
        P("blk", "col", None),
        P("col", None, None),
    )
    out_specs = (P("blk", "col", None, None, None), P())
    return jax.shard_map(
        per_device, mesh=mesh, in_specs=in_specs, out_specs=out_specs, check_vma=False
    )
```

```python
import functools

import jax
import jax.numpy as jnp
from jax import lax
from jax.experimental import pallas as pl
from jax.experimental.pallas import tpu as pltpu
from jax.sharding import PartitionSpec as P

MESH = pl.DeviceIdType.MESH
NY = 4
NL = 2
NC = 2


def far_first(n):
    return sorted(range(1, n), key=lambda d: -min(d, n - d))


def near_first(n):
    return sorted(range(1, n), key=lambda d: min(d, n - d))


def kernel(
    nz,
    nx,
    entries,
    domain,
    pattern,
    amps,
    driver,
    energy,
    gap,
    integrals,
    amps_out,
    rms_out,
    domain_s,
    gap_s,
    pattern_v,
    energy_v,
    amps_v,
    held,
    driver_v,
    denom,
    table,
    h_own,
    h_near,
    h_far,
    lanes,
    ints_out,
    ints,
    idx,
    drv,
    y_own,
    y_near,
    y_far,
    acc,
    back,
    home,
    parts,
    local_sem,
    z_send,
    z_recv,
    y_send,
    y_recv,
    t_send,
    t_recv,
    o_send,
    o_recv,
    p_send,
    p_recv,
    r_send,
    r_recv,
    m_send,
    m_recv,
):
    f32 = jnp.float32
    width = held.shape[-1]
    rows = width // nz
    nk = table.shape[0] * 2
    blk = lax.axis_index("blk")
    col = lax.axis_index("col")
    z, yh = blk // NY, blk % NY
    x, yl, core = col // (NL * NC), (col // NC) % NL, col % NC

    def at_z(d):
        return (((z + d) % nz) * NY + yh, col)

    def at_yh(d):
        return (z * NY + (yh + d) % NY, col)

    def at_y(d):
        place = (yh * NL + yl + d) % (NY * NL)
        return (z * NY + place // NL, (x * NL + place % NL) * NC + core)

    def at_x(d):
        return (blk, (((x + d) % nx) * NL + yl) * NC + core)

    def at_zc(d, e):
        return (((z + d) % nz) * NY + yh, (x * NL + yl) * NC + (core + e) % NC)

    beyond = (yh + 2 * yl - 1 + NY) % NY
    over = [(b, (x * NL + 1 - yl) * NC + core) for b in (blk, z * NY + beyond)]
    sibling = (blk, (x * NL + yl) * NC + 1 - core)
    zc_far = [(d, e) for d in far_first(nz) for e in range(NC)] + [(0, 1)]

    barrier = pltpu.get_barrier_semaphore()
    greeted = [at_zc(d, e) for d, e in zc_far]
    greeted += [at_y(d) for d in far_first(NY * NL)]
    greeted += [at_x(d) for d in far_first(nx)]
    for device in greeted:
        pl.semaphore_signal(barrier, inc=1, device_id=device, device_id_type=MESH)

    gets = []
    for src, dst in (
        (domain, domain_s),
        (amps, amps_v),
        (pattern, pattern_v),
        (integrals.at[0], table.at[col, :, pl.ds(0, width)]),
        (integrals.at[1], table.at[col, :, pl.ds(width, width)]),
        (driver, driver_v),
        (energy, energy_v),
        (gap, gap_s),
    ):
        get = pltpu.make_async_copy(src, dst, local_sem.at[len(gets)])
        get.start()
        gets.append(get)

    across = lax.broadcasted_iota(jnp.int32, (width, width), 1)
    down = lax.broadcasted_iota(jnp.int32, (width, width), 0)
    mine = pl.ds(pl.multiple_of(z * rows, rows), rows)
    gets[0].wait()
    gets[1].wait()
    for q in range(2):
        inside = (across < domain_s[0, 0, q]) & (down < domain_s[0, 0, q])
        held[q] = jnp.where(inside, amps_v[q].astype(f32), 0.0).astype(jnp.bfloat16)
    for q in range(2):
        h_own[0, q] = held[q, mine, :]

    gets[2].wait()
    lanes[...] = jnp.zeros_like(lanes)
    places = pattern_v.shape[-1]
    for p in range(2):
        tiles = pattern_v[p]
        lanes[2 * p : 2 * p + 2, 0:places] = jnp.where(tiles < 0, nk, tiles)
    spread = lanes[...]
    n = places
    while n < width:
        spread = spread + pltpu.roll(spread, n, 1)
        n *= 2
    lane = lax.broadcasted_iota(jnp.int32, lanes.shape, 1)
    sub = lax.broadcasted_iota(jnp.int32, lanes.shape, 0)
    spread = jnp.where(
        lane % NY + yh < NY,
        pltpu.roll(spread, (width - yh) % width, 1),
        pltpu.roll(spread, (width - yh + NY) % width, 1),
    )
    for d in range(nz):
        turned = pltpu.roll(spread, (width - NY * ((z + d) % nz)) % width, 1)
        turned = jnp.where(sub == 4, domain_s[0, 0, 0], jnp.where(sub == 5, domain_s[0, 0, 1], turned))
        ints_out[d] = turned

    gets[3].wait()
    gets[4].wait()
    pl.semaphore_wait(barrier, len(greeted))

    sends = []

    def send(src, dst, ssem, rsem, where_to):
        copy = pltpu.make_async_remote_copy(
            src_ref=src, dst_ref=dst, send_sem=ssem, recv_sem=rsem,
            device_id=where_to, device_id_type=MESH,
        )
        copy.start()
        sends.append(copy)

    def arrived(ref, ssem, rsem):
        pltpu.make_async_remote_copy(
            src_ref=ref, dst_ref=ref, send_sem=ssem, recv_sem=rsem,
            device_id=sibling, device_id_type=MESH,
        ).wait_recv()

    def their_rows(d):
        return pl.ds(pl.multiple_of(((z + d) % nz) * rows, rows), rows)

    order = near_first(nz)
    slot = {d: i for i, d in enumerate([0] + order)}
    near = h_near.shape[0]

    def piece(d, dy):
        if dy == 0:
            return h_own.at[slot[d]]
        if slot[d] < near:
            return h_near.at[slot[d], dy - 1]
        return h_far.at[slot[d] - near, dy - 1]

    for d in far_first(nz):
        send(held.at[:, their_rows(d), :], piece(d, 0), z_send.at[0, d], z_recv.at[0, d], at_z(d))

    def piece_out(d):
        for dy in (2, 1, 3):
            send(piece(d, 0), piece(d, dy), y_send.at[d, dy], y_recv.at[d, dy], at_yh(dy))

    def piece_from_z(d):
        arrived(piece(d, 0), z_send.at[0, d], z_recv.at[0, d])
        piece_out(d)

    def owner(dx, other, far_core):
        lo = 1 - yl if other else yl
        return (((x - dx + nx) % nx) * NL + lo) * NC + (1 - core if far_core else core)

    def unit(dx, other, far_core=0):
        return table.at[owner(dx, other, far_core)]

    def kind(dx, other, far_core=0):
        return dx + nx * other + 2 * nx * far_core

    half = width // 2

    def part(dx, other, i):
        return unit(dx, other).at[pl.ds(i * half, half), :]

    def unit_along_x():
        n = unit(0, 0)
        for d in far_first(nx):
            send(n, n, t_send.at[kind(d, 0)], t_recv.at[kind(d, 0)], at_x(d))

    def part_along_x(i):
        n = part(0, 1, i)
        arrived(n, o_send.at[i], o_recv.at[i])
        for d in far_first(nx):
            send(n, n, p_send.at[d, i], p_recv.at[d, i], at_x(d))

    def unit_to_sibling(dx, other):
        n = unit(dx, other)
        send(n, n, t_send.at[kind(dx, other, 1)], t_recv.at[kind(dx, other, 1)], sibling)

    def unit_in(dx, other, far_core=0):
        n = kind(dx, other, far_core)
        arrived(unit(dx, other, far_core), t_send.at[n], t_recv.at[n])

    def unit_from_x(dx, other):
        if other:
            for i in range(2):
                arrived(part(dx, 1, i), p_send.at[dx, i], p_recv.at[dx, i])
        else:
            unit_in(dx, 0)
        unit_to_sibling(dx, other)

    for i, device in enumerate(over):
        send(part(0, 0, i), part(0, 0, i), o_send.at[i], o_recv.at[i], device)
    unit_along_x()
    piece_out(0)
    unit_to_sibling(0, 0)
    for d in far_first(nz):
        send(ints_out.at[d], ints.at[z], z_send.at[1, d], z_recv.at[1, d], at_z(d))
    gets[5].wait()
    for d in far_first(nz):
        send(driver_v.at[:, their_rows(d), :], drv.at[z], z_send.at[2, d], z_recv.at[2, d], at_z(d))
    for p in range(2):
        drv[z, p] = driver_v[p, mine, :]
    ints[z] = ints_out[0]
    for y in (y_own, y_near, y_far):
        y[:, nk] = jnp.zeros((y.shape[0], *y.shape[2:]), f32)

    for d in order[:4]:
        piece_from_z(d)
    part_along_x(0)
    part_along_x(1)
    unit_to_sibling(0, 1)
    for d in order[4:6]:
        piece_from_z(d)
    for d in near_first(nx)[:2]:
        unit_from_x(d, 0)
    for d in order[6:]:
        piece_from_z(d)
    for d in near_first(nx)[2:]:
        unit_from_x(d, 0)

    for d in order:
        arrived(ints.at[(z - d + nz) % nz], z_send.at[1, d], z_recv.at[1, d])
    get_idx = pltpu.make_async_copy(ints, idx, local_sem.at[len(gets)])
    get_idx.start()
    gets[6].wait()
    gets[7].wait()
    for p in range(2):
        own = jnp.broadcast_to(energy_v[0, 0, p : p + 1, :], (width, width))
        turned = jnp.sum(jnp.where(across == down, own, 0.0), axis=1, keepdims=True)
        denom[p] = turned + own + gap_s[0, 0, p]

    def rows_of(h):
        count = h.size // width
        return h[...].reshape(count, width)

    def products(lhs, y, dx, other, far_core):
        o = owner(dx, other, far_core)
        both = jnp.dot(lhs, table[o], preferred_element_type=f32)
        y[:, 2 * o] = both[:, :width].reshape(y.shape[0], rows, width)
        y[:, 2 * o + 1] = both[:, width:].reshape(y.shape[0], rows, width)

    def add_up(pieces, y, first):
        def step(zo, carry):
            for p in range(2):
                total = None if first else acc[zo * 2 + p]
                for i, (d, dy) in enumerate(pieces):
                    place = ((nz - d) % nz) * NY + (NY - dy) % NY
                    for q in range(2):
                        k = idx[zo, p * 2 + q, place]
                        term = y[i * 2 + q, k]
                        total = term if total is None else total + term
                acc[zo * 2 + p] = total
            return carry

        lax.fori_loop(0, nz, step, 0)

    early = [(0, 0), (0, 1)] + [(dx, 0) for dx in near_first(nx)]
    late = [(dx, 1) for dx in near_first(nx)]
    ahead = [0] + order
    pieces_near = [(d, dy) for d in ahead[:near] for dy in range(1, NY)]
    pieces_far = [(d, dy) for d in ahead[near:] for dy in range(1, NY)]

    def pieces_in(pieces):
        for d, dy in pieces:
            arrived(piece(d, dy), y_send.at[d, dy], y_recv.at[d, dy])

    own = rows_of(h_own)
    for n in early:
        products(own, y_own, *n, 0)
    for n in early:
        unit_in(*n, 1)
        products(own, y_own, *n, 1)
    for n in late:
        unit_from_x(*n)
    for n in late:
        products(own, y_own, *n, 0)
    pieces_in(pieces_near)
    beside = rows_of(h_near)
    for far_core in range(2):
        for n in early:
            products(beside, y_near, *n, far_core)
    for n in late:
        products(beside, y_near, *n, 0)
    for n in late:
        unit_in(*n, 1)
        products(own, y_own, *n, 1)
        products(beside, y_near, *n, 1)
    get_idx.wait()
    add_up([(d, 0) for d in ahead], y_own, True)
    add_up(pieces_near, y_near, False)
    pieces_in(pieces_far)
    beyond_rows = rows_of(h_far)
    for far_core in range(2):
        for n in early + late:
            products(beyond_rows, y_far, *n, far_core)
    add_up(pieces_far, y_far, False)

    for d in order:
        arrived(drv.at[(z - d + nz) % nz], z_send.at[2, d], z_recv.at[2, d])
    below = lax.broadcasted_iota(jnp.int32, (rows, width), 0) + z * rows
    aside = lax.broadcasted_iota(jnp.int32, (rows, width), 1)
    squares = jnp.zeros((rows, width), f32)
    for zo in range(nz):
        for p in range(2):
            limit = idx[zo, 4 + p, 0]
            inside = (below < limit) & (aside < limit)
            value = jnp.where(inside, drv[zo, p] + acc[zo * 2 + p], 0.0)
            back[zo, p] = value
            squares = squares + value * value
    squares = jnp.sum(squares, axis=0, keepdims=True)

    def stage_out(i, place, peers, value):
        parts[i, place] = value
        for j, device in enumerate(peers):
            send(parts.at[i, place], parts.at[i, place], m_send.at[i, j], m_recv.at[i, j], device)

    def stage_in(i, places):
        for j, place in reversed(list(enumerate(places))):
            arrived(parts.at[i, place], m_send.at[i, j], m_recv.at[i, j])
        total = parts[i, 0]
        for j in range(1, len(places) + 1):
            total = total + parts[i, j]
        return total

    yy, ny = yh * NL + yl, NY * NL
    stage_out(0, z * NC + core, [at_zc(d, e) for d, e in zc_far], squares)
    for d in far_first(nz):
        send(back.at[(z + d) % nz], home.at[:, mine, :], r_send.at[d], r_recv.at[d], at_z(d))
    for p in range(2):
        home[p, mine, :] = back[z, p]
    total = stage_in(0, [((z - d + nz) % nz) * NC + (core + e) % NC for d, e in zc_far])
    stage_out(1, yy, [at_y(d) for d in far_first(ny)], total)
    total = stage_in(1, [(yy - d + ny) % ny for d in far_first(ny)])
    stage_out(2, x, [at_x(d) for d in far_first(nx)], total)
    for d in order:
        theirs = pl.ds(pl.multiple_of(((z - d + nz) % nz) * rows, rows), rows)
        arrived(home.at[:, theirs, :], r_send.at[d], r_recv.at[d])
    for p in range(2):
        amps_out[p] = held[p].astype(f32) + home[p] / denom[p]
    for copy in sends:
        copy.wait_send()
    total = stage_in(2, [(x - d + nx) % nx for d in far_first(nx)])
    rms_out[0, 0] = jnp.max(jnp.sqrt(jnp.full((8, width), jnp.sum(total) / entries, f32)))


def per_device(amps, driver, pattern, domain, virt_energy, pair_gap, integrals):
    width = amps.shape[-1]
    per_block = amps.shape[2]
    nz = lax.axis_size("blk") // NY
    nx = lax.axis_size("col") // (NL * NC)
    rows_of = width // nz
    owners = lax.axis_size("col")
    nk = owners * integrals.shape[0]
    entries = float(lax.axis_size("blk") * owners * per_block * width * width)
    near = 3
    dma = pltpu.SemaphoreType.DMA
    in_hbm = pl.BlockSpec(memory_space=pltpu.HBM)
    tile = (width, width)
    operands = (
        domain,
        jnp.swapaxes(pattern[0, 0], 1, 2),
        amps[0, 0],
        driver[0, 0],
        virt_energy,
        pair_gap,
        integrals,
    )
    new_amps, rms = pl.pallas_call(
        functools.partial(kernel, nz, nx, entries),
        out_shape=(
            jax.ShapeDtypeStruct((per_block, *tile), jnp.float32),
            jax.ShapeDtypeStruct((1, 1), jnp.float32),
        ),
        in_specs=[in_hbm] * 7,
        out_specs=(pl.BlockSpec(memory_space=pltpu.VMEM), pl.BlockSpec(memory_space=pltpu.SMEM)),
        scratch_shapes=[
            pltpu.SMEM((1, 1, 2), jnp.int32),
            pltpu.SMEM((1, 1, 2), jnp.float32),
            pltpu.VMEM((2, 2, pattern.shape[3]), jnp.int32),
            pltpu.VMEM((1, 1, 2, width), jnp.float32),
            pltpu.VMEM((2, *tile), jnp.bfloat16),
            pltpu.VMEM((2, *tile), jnp.bfloat16),
            pltpu.VMEM((2, *tile), jnp.float32),
            pltpu.VMEM((2, *tile), jnp.float32),
            pltpu.VMEM((owners, width, 2 * width), jnp.bfloat16),
            pltpu.VMEM((nz, 2, rows_of, width), jnp.bfloat16),
            pltpu.VMEM((near, NY - 1, 2, rows_of, width), jnp.bfloat16),
            pltpu.VMEM((nz - near, NY - 1, 2, rows_of, width), jnp.bfloat16),
            pltpu.VMEM((8, width), jnp.int32),
            pltpu.VMEM((nz, 8, width), jnp.int32),
            pltpu.VMEM((nz, 8, width), jnp.int32),
            pltpu.SMEM((nz, 8, width), jnp.int32),
            pltpu.VMEM((nz, 2, rows_of, width), jnp.float32),
            pltpu.VMEM((nz * 2, nk + 1, rows_of, width), jnp.float32),
            pltpu.VMEM((near * (NY - 1) * 2, nk + 1, rows_of, width), jnp.float32),
            pltpu.VMEM(((nz - near) * (NY - 1) * 2, nk + 1, rows_of, width), jnp.float32),
            pltpu.VMEM((nz * 2, rows_of, width), jnp.float32),
            pltpu.VMEM((nz, 2, rows_of, width), jnp.float32),
            pltpu.VMEM((2, *tile), jnp.float32),
            pltpu.VMEM((3, nz * NC, 1, width), jnp.float32),
            dma((9,)),
            dma((3, nz)),
            dma((3, nz)),
            dma((nz, NY)),
            dma((nz, NY)),
            dma((4 * nx,)),
            dma((4 * nx,)),
            dma((2,)),
            dma((2,)),
            dma((nx, 2)),
            dma((nx, 2)),
            dma((nz,)),
            dma((nz,)),
            dma((3, nz * NC)),
            dma((3, nz * NC)),
        ],
        compiler_params=pltpu.CompilerParams(
            collective_id=0, has_side_effects=True, vmem_limit_bytes=40 * 1024 * 1024
        ),
    )(
        *(pltpu.with_memory_space_constraint(a, pltpu.HBM) for a in operands)
    )
    return (new_amps[None, None], rms.reshape(()))


def solution(mesh):
    in_specs = (
        P("blk", "col", None, None, None),
        P("blk", "col", None, None, None),
        P("blk", "col", None, None, None),
        P("blk", "col", None),
        P("blk", "col", None, None),
        P("blk", "col", None),
        P("col", None, None),
    )
    out_specs = (P("blk", "col", None, None, None), P())
    return jax.shard_map(
        per_device, mesh=mesh, in_specs=in_specs, out_specs=out_specs, check_vma=False
    )
```

```python
import functools

import jax
import jax.numpy as jnp
from jax import lax
from jax.experimental import pallas as pl
from jax.experimental.pallas import tpu as pltpu
from jax.sharding import PartitionSpec as P

MESH = pl.DeviceIdType.MESH
NY = 4
NL = 2
NC = 2


def far_first(n):
    return sorted(range(1, n), key=lambda d: -min(d, n - d))


def near_first(n):
    return sorted(range(1, n), key=lambda d: min(d, n - d))


def kernel(
    nz,
    nx,
    entries,
    domain,
    pattern,
    amps,
    driver,
    energy,
    gap,
    integrals,
    amps_out,
    rms_out,
    domain_s,
    gap_s,
    pattern_v,
    energy_v,
    amps_v,
    held,
    driver_v,
    denom,
    table,
    h_own,
    h_near,
    h_far,
    lanes,
    ints_out,
    ints,
    idx,
    drv,
    y_own,
    y_near,
    y_far,
    acc,
    back,
    home,
    parts,
    local_sem,
    z_send,
    z_recv,
    y_send,
    y_recv,
    t_send,
    t_recv,
    o_send,
    o_recv,
    p_send,
    p_recv,
    r_send,
    r_recv,
    m_send,
    m_recv,
):
    f32 = jnp.float32
    width = held.shape[-1]
    rows = width // nz
    nk = table.shape[0] * 2
    blk = lax.axis_index("blk")
    col = lax.axis_index("col")
    z, yh = blk // NY, blk % NY
    x, yl, core = col // (NL * NC), (col // NC) % NL, col % NC

    def at_z(d):
        return (((z + d) % nz) * NY + yh, col)

    def at_yh(d):
        return (z * NY + (yh + d) % NY, col)

    def at_y(d):
        place = (yh * NL + yl + d) % (NY * NL)
        return (z * NY + place // NL, (x * NL + place % NL) * NC + core)

    def at_x(d):
        return (blk, (((x + d) % nx) * NL + yl) * NC + core)

    def at_zc(d, e):
        return (((z + d) % nz) * NY + yh, (x * NL + yl) * NC + (core + e) % NC)

    def at_yx(d, e):
        place = (yh * NL + yl + d) % (NY * NL)
        return (z * NY + place // NL, (((x + e) % nx) * NL + place % NL) * NC + core)

    beyond = (yh + 2 * yl - 1 + NY) % NY
    over = [(b, (x * NL + 1 - yl) * NC + core) for b in (blk, z * NY + beyond)]
    sibling = (blk, (x * NL + yl) * NC + 1 - core)
    zc_far = [(d, e) for d in far_first(nz) for e in range(NC)] + [(0, 1)]
    yx_far = sorted(
        [(d, e) for d in range(NY * NL) for e in range(nx) if d or e],
        key=lambda n: -min(n[0], NY * NL - n[0]) - min(n[1], nx - n[1]),
    )

    barrier = pltpu.get_barrier_semaphore()
    greeted = [at_zc(d, e) for d, e in zc_far]
    greeted += [at_yx(d, e) for d, e in yx_far]
    for device in greeted:
        pl.semaphore_signal(barrier, inc=1, device_id=device, device_id_type=MESH)

    gets = []
    for src, dst in (
        (domain, domain_s),
        (amps, amps_v),
        (pattern, pattern_v),
        (integrals.at[0], table.at[col, :, pl.ds(0, width)]),
        (integrals.at[1], table.at[col, :, pl.ds(width, width)]),
        (driver, driver_v),
        (energy, energy_v),
        (gap, gap_s),
    ):
        get = pltpu.make_async_copy(src, dst, local_sem.at[len(gets)])
        get.start()
        gets.append(get)

    across = lax.broadcasted_iota(jnp.int32, (width, width), 1)
    down = lax.broadcasted_iota(jnp.int32, (width, width), 0)
    mine = pl.ds(pl.multiple_of(z * rows, rows), rows)
    gets[0].wait()
    gets[1].wait()
    for q in range(2):
        inside = (across < domain_s[0, 0, q]) & (down < domain_s[0, 0, q])
        held[q] = jnp.where(inside, amps_v[q].astype(f32), 0.0).astype(jnp.bfloat16)
    for q in range(2):
        h_own[0, q] = held[q, mine, :]

    gets[2].wait()
    lanes[...] = jnp.zeros_like(lanes)
    places = pattern_v.shape[-1]
    for p in range(2):
        tiles = pattern_v[p]
        lanes[2 * p : 2 * p + 2, 0:places] = jnp.where(tiles < 0, nk, tiles)
    spread = lanes[...]
    n = places
    while n < width:
        spread = spread + pltpu.roll(spread, n, 1)
        n *= 2
    lane = lax.broadcasted_iota(jnp.int32, lanes.shape, 1)
    sub = lax.broadcasted_iota(jnp.int32, lanes.shape, 0)
    spread = jnp.where(
        lane % NY + yh < NY,
        pltpu.roll(spread, (width - yh) % width, 1),
        pltpu.roll(spread, (width - yh + NY) % width, 1),
    )
    for d in range(nz):
        turned = pltpu.roll(spread, (width - NY * ((z + d) % nz)) % width, 1)
        turned = jnp.where(sub == 4, domain_s[0, 0, 0], jnp.where(sub == 5, domain_s[0, 0, 1], turned))
        ints_out[d] = turned

    gets[3].wait()
    gets[4].wait()
    pl.semaphore_wait(barrier, len(greeted))

    sends = []

    def send(src, dst, ssem, rsem, where_to):
        copy = pltpu.make_async_remote_copy(
            src_ref=src, dst_ref=dst, send_sem=ssem, recv_sem=rsem,
            device_id=where_to, device_id_type=MESH,
        )
        copy.start()
        sends.append(copy)

    def arrived(ref, ssem, rsem):
        pltpu.make_async_remote_copy(
            src_ref=ref, dst_ref=ref, send_sem=ssem, recv_sem=rsem,
            device_id=sibling, device_id_type=MESH,
        ).wait_recv()

    def their_rows(d):
        return pl.ds(pl.multiple_of(((z + d) % nz) * rows, rows), rows)

    order = near_first(nz)
    slot = {d: i for i, d in enumerate([0] + order)}
    near = h_near.shape[0]

    def piece(d, dy):
        if dy == 0:
            return h_own.at[slot[d]]
        if slot[d] < near:
            return h_near.at[slot[d], dy - 1]
        return h_far.at[slot[d] - near, dy - 1]

    for d in far_first(nz):
        send(held.at[:, their_rows(d), :], piece(d, 0), z_send.at[0, d], z_recv.at[0, d], at_z(d))

    def piece_out(d):
        for dy in (2, 1, 3):
            send(piece(d, 0), piece(d, dy), y_send.at[d, dy], y_recv.at[d, dy], at_yh(dy))

    def piece_from_z(d):
        arrived(piece(d, 0), z_send.at[0, d], z_recv.at[0, d])
        piece_out(d)

    def owner(dx, other, far_core):
        lo = 1 - yl if other else yl
        return (((x - dx + nx) % nx) * NL + lo) * NC + (1 - core if far_core else core)

    def unit(dx, other, far_core=0):
        return table.at[owner(dx, other, far_core)]

    def kind(dx, other, far_core=0):
        return dx + nx * other + 2 * nx * far_core

    half = width // 2

    def part(dx, other, i):
        return unit(dx, other).at[pl.ds(i * half, half), :]

    def unit_along_x():
        n = unit(0, 0)
        for d in far_first(nx):
            send(n, n, t_send.at[kind(d, 0)], t_recv.at[kind(d, 0)], at_x(d))

    def part_along_x(i):
        n = part(0, 1, i)
        arrived(n, o_send.at[i], o_recv.at[i])
        for d in far_first(nx):
            send(n, n, p_send.at[d, i], p_recv.at[d, i], at_x(d))

    def unit_to_sibling(dx, other):
        n = unit(dx, other)
        send(n, n, t_send.at[kind(dx, other, 1)], t_recv.at[kind(dx, other, 1)], sibling)

    def unit_in(dx, other, far_core=0):
        n = kind(dx, other, far_core)
        arrived(unit(dx, other, far_core), t_send.at[n], t_recv.at[n])

    def unit_from_x(dx, other):
        if other:
            for i in range(2):
                arrived(part(dx, 1, i), p_send.at[dx, i], p_recv.at[dx, i])
        else:
            unit_in(dx, 0)
        unit_to_sibling(dx, other)

    for i, device in enumerate(over):
        send(part(0, 0, i), part(0, 0, i), o_send.at[i], o_recv.at[i], device)
    unit_along_x()
    piece_out(0)
    unit_to_sibling(0, 0)
    for d in far_first(nz):
        send(ints_out.at[d], ints.at[z], z_send.at[1, d], z_recv.at[1, d], at_z(d))
    gets[5].wait()
    for d in far_first(nz):
        send(driver_v.at[:, their_rows(d), :], drv.at[z], z_send.at[2, d], z_recv.at[2, d], at_z(d))
    for p in range(2):
        drv[z, p] = driver_v[p, mine, :]
    ints[z] = ints_out[0]
    for y in (y_own, y_near, y_far):
        y[:, nk] = jnp.zeros((y.shape[0], *y.shape[2:]), f32)

    for d in order[:4]:
        piece_from_z(d)
    part_along_x(0)
    part_along_x(1)
    unit_to_sibling(0, 1)
    for d in order[4:6]:
        piece_from_z(d)
    for d in near_first(nx)[:2]:
        unit_from_x(d, 0)
    for d in order[6:]:
        piece_from_z(d)
    for d in near_first(nx)[2:]:
        unit_from_x(d, 0)

    for d in order:
        arrived(ints.at[(z - d + nz) % nz], z_send.at[1, d], z_recv.at[1, d])
    get_idx = pltpu.make_async_copy(ints, idx, local_sem.at[len(gets)])
    get_idx.start()
    gets[6].wait()
    gets[7].wait()
    for p in range(2):
        own = jnp.broadcast_to(energy_v[0, 0, p : p + 1, :], (width, width))
        turned = jnp.sum(jnp.where(across == down, own, 0.0), axis=1, keepdims=True)
        denom[p] = turned + own + gap_s[0, 0, p]

    def rows_of(h):
        count = h.size // width
        return h[...].reshape(count, width)

    def products(lhs, y, dx, other, far_core):
        o = owner(dx, other, far_core)
        both = jnp.dot(lhs, table[o], preferred_element_type=f32)
        y[:, 2 * o] = both[:, :width].reshape(y.shape[0], rows, width)
        y[:, 2 * o + 1] = both[:, width:].reshape(y.shape[0], rows, width)

    def add_up(pieces, y, first):
        def step(zo, carry):
            for p in range(2):
                total = None if first else acc[zo * 2 + p]
                for i, (d, dy) in enumerate(pieces):
                    place = ((nz - d) % nz) * NY + (NY - dy) % NY
                    for q in range(2):
                        k = idx[zo, p * 2 + q, place]
                        term = y[i * 2 + q, k]
                        total = term if total is None else total + term
                acc[zo * 2 + p] = total
            return carry

        lax.fori_loop(0, nz, step, 0)

    early = [(0, 0), (0, 1)] + [(dx, 0) for dx in near_first(nx)]
    late = [(dx, 1) for dx in near_first(nx)]
    ahead = [0] + order
    pieces_near = [(d, dy) for d in ahead[:near] for dy in range(1, NY)]
    pieces_far = [(d, dy) for d in ahead[near:] for dy in range(1, NY)]

    def pieces_in(pieces):
        for d, dy in pieces:
            arrived(piece(d, dy), y_send.at[d, dy], y_recv.at[d, dy])

    own = rows_of(h_own)
    for n in early:
        products(own, y_own, *n, 0)
    for n in early:
        unit_in(*n, 1)
        products(own, y_own, *n, 1)
    for n in late:
        unit_from_x(*n)
    for n in late:
        products(own, y_own, *n, 0)
    pieces_in(pieces_near)
    beside = rows_of(h_near)
    for far_core in range(2):
        for n in early:
            products(beside, y_near, *n, far_core)
    for n in late:
        products(beside, y_near, *n, 0)
    for n in late:
        unit_in(*n, 1)
        products(own, y_own, *n, 1)
        products(beside, y_near, *n, 1)
    get_idx.wait()
    add_up([(d, 0) for d in ahead], y_own, True)
    add_up(pieces_near, y_near, False)
    pieces_in(pieces_far)
    beyond_rows = rows_of(h_far)
    for far_core in range(2):
        for n in early + late:
            products(beyond_rows, y_far, *n, far_core)
    add_up(pieces_far, y_far, False)

    for d in order:
        arrived(drv.at[(z - d + nz) % nz], z_send.at[2, d], z_recv.at[2, d])
    below = lax.broadcasted_iota(jnp.int32, (rows, width), 0) + z * rows
    aside = lax.broadcasted_iota(jnp.int32, (rows, width), 1)
    squares = jnp.zeros((rows, width), f32)
    for zo in range(nz):
        for p in range(2):
            limit = idx[zo, 4 + p, 0]
            inside = (below < limit) & (aside < limit)
            value = jnp.where(inside, drv[zo, p] + acc[zo * 2 + p], 0.0)
            back[zo, p] = value
            squares = squares + value * value
    squares = jnp.sum(squares, axis=0, keepdims=True)

    def stage_out(i, place, peers, value):
        parts[i, place] = value
        for j, device in enumerate(peers):
            send(parts.at[i, place], parts.at[i, place], m_send.at[i, j], m_recv.at[i, j], device)

    def stage_in(i, places):
        for j, place in reversed(list(enumerate(places))):
            arrived(parts.at[i, place], m_send.at[i, j], m_recv.at[i, j])
        total = parts[i, 0]
        for j in range(1, len(places) + 1):
            total = total + parts[i, j]
        return total

    yy, ny = yh * NL + yl, NY * NL
    stage_out(0, z * NC + core, [at_zc(d, e) for d, e in zc_far], squares)
    for d in far_first(nz):
        send(back.at[(z + d) % nz], home.at[:, mine, :], r_send.at[d], r_recv.at[d], at_z(d))
    for p in range(2):
        home[p, mine, :] = back[z, p]
    total = stage_in(0, [((z - d + nz) % nz) * NC + (core + e) % NC for d, e in zc_far])
    stage_out(1, yy * nx + x, [at_yx(d, e) for d, e in yx_far], total)
    for d in order:
        theirs = pl.ds(pl.multiple_of(((z - d + nz) % nz) * rows, rows), rows)
        arrived(home.at[:, theirs, :], r_send.at[d], r_recv.at[d])
    for p in range(2):
        amps_out[p] = held[p].astype(f32) + home[p] / denom[p]
    for copy in sends:
        copy.wait_send()
    total = stage_in(1, [((yy - d + ny) % ny) * nx + (x - e + nx) % nx for d, e in yx_far])
    rms_out[0, 0] = jnp.max(jnp.sqrt(jnp.full((8, width), jnp.sum(total) / entries, f32)))


def per_device(amps, driver, pattern, domain, virt_energy, pair_gap, integrals):
    width = amps.shape[-1]
    per_block = amps.shape[2]
    nz = lax.axis_size("blk") // NY
    nx = lax.axis_size("col") // (NL * NC)
    rows_of = width // nz
    owners = lax.axis_size("col")
    nk = owners * integrals.shape[0]
    entries = float(lax.axis_size("blk") * owners * per_block * width * width)
    near = 3
    sums = max(nz * NC, NY * NL * nx)
    dma = pltpu.SemaphoreType.DMA
    in_hbm = pl.BlockSpec(memory_space=pltpu.HBM)
    tile = (width, width)
    operands = (
        domain,
        jnp.swapaxes(pattern[0, 0], 1, 2),
        amps[0, 0],
        driver[0, 0],
        virt_energy,
        pair_gap,
        integrals,
    )
    new_amps, rms = pl.pallas_call(
        functools.partial(kernel, nz, nx, entries),
        out_shape=(
            jax.ShapeDtypeStruct((per_block, *tile), jnp.float32),
            jax.ShapeDtypeStruct((1, 1), jnp.float32),
        ),
        in_specs=[in_hbm] * 7,
        out_specs=(pl.BlockSpec(memory_space=pltpu.VMEM), pl.BlockSpec(memory_space=pltpu.SMEM)),
        scratch_shapes=[
            pltpu.SMEM((1, 1, 2), jnp.int32),
            pltpu.SMEM((1, 1, 2), jnp.float32),
            pltpu.VMEM((2, 2, pattern.shape[3]), jnp.int32),
            pltpu.VMEM((1, 1, 2, width), jnp.float32),
            pltpu.VMEM((2, *tile), jnp.bfloat16),
            pltpu.VMEM((2, *tile), jnp.bfloat16),
            pltpu.VMEM((2, *tile), jnp.float32),
            pltpu.VMEM((2, *tile), jnp.float32),
            pltpu.VMEM((owners, width, 2 * width), jnp.bfloat16),
            pltpu.VMEM((nz, 2, rows_of, width), jnp.bfloat16),
            pltpu.VMEM((near, NY - 1, 2, rows_of, width), jnp.bfloat16),
            pltpu.VMEM((nz - near, NY - 1, 2, rows_of, width), jnp.bfloat16),
            pltpu.VMEM((8, width), jnp.int32),
            pltpu.VMEM((nz, 8, width), jnp.int32),
            pltpu.VMEM((nz, 8, width), jnp.int32),
            pltpu.SMEM((nz, 8, width), jnp.int32),
            pltpu.VMEM((nz, 2, rows_of, width), jnp.float32),
            pltpu.VMEM((nz * 2, nk + 1, rows_of, width), jnp.float32),
            pltpu.VMEM((near * (NY - 1) * 2, nk + 1, rows_of, width), jnp.float32),
            pltpu.VMEM(((nz - near) * (NY - 1) * 2, nk + 1, rows_of, width), jnp.float32),
            pltpu.VMEM((nz * 2, rows_of, width), jnp.float32),
            pltpu.VMEM((nz, 2, rows_of, width), jnp.float32),
            pltpu.VMEM((2, *tile), jnp.float32),
            pltpu.VMEM((2, sums, 1, width), jnp.float32),
            dma((9,)),
            dma((3, nz)),
            dma((3, nz)),
            dma((nz, NY)),
            dma((nz, NY)),
            dma((4 * nx,)),
            dma((4 * nx,)),
            dma((2,)),
            dma((2,)),
            dma((nx, 2)),
            dma((nx, 2)),
            dma((nz,)),
            dma((nz,)),
            dma((2, sums)),
            dma((2, sums)),
        ],
        compiler_params=pltpu.CompilerParams(
            collective_id=0, has_side_effects=True, vmem_limit_bytes=40 * 1024 * 1024
        ),
    )(
        *(pltpu.with_memory_space_constraint(a, pltpu.HBM) for a in operands)
    )
    return (new_amps[None, None], rms.reshape(()))


def solution(mesh):
    in_specs = (
        P("blk", "col", None, None, None),
        P("blk", "col", None, None, None),
        P("blk", "col", None, None, None),
        P("blk", "col", None),
        P("blk", "col", None, None),
        P("blk", "col", None),
        P("col", None, None),
    )
    out_specs = (P("blk", "col", None, None, None), P())
    return jax.shard_map(
        per_device, mesh=mesh, in_specs=in_specs, out_specs=out_specs, check_vma=False
    )
```

```python
import functools

import jax
import jax.numpy as jnp
from jax import lax
from jax.experimental import pallas as pl
from jax.experimental.pallas import tpu as pltpu
from jax.sharding import PartitionSpec as P

MESH = pl.DeviceIdType.MESH
NY = 4
NL = 2
NC = 2


def far_first(n):
    return sorted(range(1, n), key=lambda d: -min(d, n - d))


def near_first(n):
    return sorted(range(1, n), key=lambda d: min(d, n - d))


def kernel(
    nz,
    nx,
    entries,
    domain,
    pattern,
    amps,
    driver,
    energy,
    gap,
    integrals,
    amps_out,
    rms_out,
    domain_s,
    gap_s,
    pattern_v,
    energy_v,
    amps_v,
    held,
    driver_v,
    denom,
    table,
    h_own,
    h_near,
    h_far,
    lanes,
    ints_out,
    ints,
    idx,
    drv,
    y_own,
    y_near,
    y_far,
    acc,
    back,
    home,
    parts,
    local_sem,
    z_send,
    z_recv,
    y_send,
    y_recv,
    t_send,
    t_recv,
    o_send,
    o_recv,
    p_send,
    p_recv,
    r_send,
    r_recv,
    m_send,
    m_recv,
):
    f32 = jnp.float32
    width = held.shape[-1]
    rows = width // nz
    nk = table.shape[0] * 2
    blk = lax.axis_index("blk")
    col = lax.axis_index("col")
    z, yh = blk // NY, blk % NY
    x, yl, core = col // (NL * NC), (col // NC) % NL, col % NC

    def at_z(d):
        return (((z + d) % nz) * NY + yh, col)

    def at_yh(d):
        return (z * NY + (yh + d) % NY, col)

    def at_y(d):
        place = (yh * NL + yl + d) % (NY * NL)
        return (z * NY + place // NL, (x * NL + place % NL) * NC + core)

    def at_x(d):
        return (blk, (((x + d) % nx) * NL + yl) * NC + core)

    def at_zc(d, e):
        return (((z + d) % nz) * NY + yh, (x * NL + yl) * NC + (core + e) % NC)

    def at_yx(d, e):
        place = (yh * NL + yl + d) % (NY * NL)
        return (z * NY + place // NL, (((x + e) % nx) * NL + place % NL) * NC + core)

    beyond = (yh + 2 * yl - 1 + NY) % NY
    over = [(b, (x * NL + 1 - yl) * NC + core) for b in (blk, z * NY + beyond)]
    sibling = (blk, (x * NL + yl) * NC + 1 - core)
    zc_far = [(d, e) for d in far_first(nz) for e in range(NC)] + [(0, 1)]
    yx_far = sorted(
        [(d, e) for d in range(NY * NL) for e in range(nx) if d or e],
        key=lambda n: -min(n[0], NY * NL - n[0]) - min(n[1], nx - n[1]),
    )

    barrier = pltpu.get_barrier_semaphore()
    greeted = [at_zc(d, e) for d, e in zc_far]
    greeted += [at_y(d) for d in far_first(NY * NL)]
    greeted += [at_x(d) for d in far_first(nx)]
    for device in greeted:
        pl.semaphore_signal(barrier, inc=1, device_id=device, device_id_type=MESH)

    gets = []
    for src, dst in (
        (domain, domain_s),
        (amps, amps_v),
        (pattern, pattern_v),
        (integrals.at[0], table.at[col, :, pl.ds(0, width)]),
        (integrals.at[1], table.at[col, :, pl.ds(width, width)]),
        (driver, driver_v),
        (energy, energy_v),
        (gap, gap_s),
    ):
        get = pltpu.make_async_copy(src, dst, local_sem.at[len(gets)])
        get.start()
        gets.append(get)

    across = lax.broadcasted_iota(jnp.int32, (width, width), 1)
    down = lax.broadcasted_iota(jnp.int32, (width, width), 0)
    mine = pl.ds(pl.multiple_of(z * rows, rows), rows)
    gets[0].wait()
    gets[1].wait()
    for q in range(2):
        inside = (across < domain_s[0, 0, q]) & (down < domain_s[0, 0, q])
        held[q] = jnp.where(inside, amps_v[q].astype(f32), 0.0).astype(jnp.bfloat16)
    for q in range(2):
        h_own[0, q] = held[q, mine, :]

    gets[2].wait()
    lanes[...] = jnp.zeros_like(lanes)
    places = pattern_v.shape[-1]
    for p in range(2):
        tiles = pattern_v[p]
        lanes[2 * p : 2 * p + 2, 0:places] = jnp.where(tiles < 0, nk, tiles)
    spread = lanes[...]
    n = places
    while n < width:
        spread = spread + pltpu.roll(spread, n, 1)
        n *= 2
    lane = lax.broadcasted_iota(jnp.int32, lanes.shape, 1)
    sub = lax.broadcasted_iota(jnp.int32, lanes.shape, 0)
    spread = jnp.where(
        lane % NY + yh < NY,
        pltpu.roll(spread, (width - yh) % width, 1),
        pltpu.roll(spread, (width - yh + NY) % width, 1),
    )
    for d in range(nz):
        turned = pltpu.roll(spread, (width - NY * ((z + d) % nz)) % width, 1)
        turned = jnp.where(sub == 4, domain_s[0, 0, 0], jnp.where(sub == 5, domain_s[0, 0, 1], turned))
        ints_out[d] = turned

    gets[3].wait()
    gets[4].wait()
    pl.semaphore_wait(barrier, len(greeted))

    sends = []

    def send(src, dst, ssem, rsem, where_to):
        copy = pltpu.make_async_remote_copy(
            src_ref=src, dst_ref=dst, send_sem=ssem, recv_sem=rsem,
            device_id=where_to, device_id_type=MESH,
        )
        copy.start()
        sends.append(copy)

    def arrived(ref, ssem, rsem):
        pltpu.make_async_remote_copy(
            src_ref=ref, dst_ref=ref, send_sem=ssem, recv_sem=rsem,
            device_id=sibling, device_id_type=MESH,
        ).wait_recv()

    def their_rows(d):
        return pl.ds(pl.multiple_of(((z + d) % nz) * rows, rows), rows)

    order = near_first(nz)
    slot = {d: i for i, d in enumerate([0] + order)}
    near = h_near.shape[0]

    def piece(d, dy):
        if dy == 0:
            return h_own.at[slot[d]]
        if slot[d] < near:
            return h_near.at[slot[d], dy - 1]
        return h_far.at[slot[d] - near, dy - 1]

    for d in far_first(nz):
        send(held.at[:, their_rows(d), :], piece(d, 0), z_send.at[0, d], z_recv.at[0, d], at_z(d))

    def piece_out(d):
        for dy in (2, 1, 3):
            send(piece(d, 0), piece(d, dy), y_send.at[d, dy], y_recv.at[d, dy], at_yh(dy))

    def piece_from_z(d):
        arrived(piece(d, 0), z_send.at[0, d], z_recv.at[0, d])
        piece_out(d)

    def owner(dx, other, far_core):
        lo = 1 - yl if other else yl
        return (((x - dx + nx) % nx) * NL + lo) * NC + (1 - core if far_core else core)

    def unit(dx, other, far_core=0):
        return table.at[owner(dx, other, far_core)]

    def kind(dx, other, far_core=0):
        return dx + nx * other + 2 * nx * far_core

    half = width // 2

    def part(dx, other, i):
        return unit(dx, other).at[pl.ds(i * half, half), :]

    def unit_along_x():
        n = unit(0, 0)
        for d in far_first(nx):
            send(n, n, t_send.at[kind(d, 0)], t_recv.at[kind(d, 0)], at_x(d))

    def part_along_x(i):
        n = part(0, 1, i)
        arrived(n, o_send.at[i], o_recv.at[i])
        for d in far_first(nx):
            send(n, n, p_send.at[d, i], p_recv.at[d, i], at_x(d))

    def unit_to_sibling(dx, other):
        n = unit(dx, other)
        send(n, n, t_send.at[kind(dx, other, 1)], t_recv.at[kind(dx, other, 1)], sibling)

    def unit_in(dx, other, far_core=0):
        n = kind(dx, other, far_core)
        arrived(unit(dx, other, far_core), t_send.at[n], t_recv.at[n])

    def unit_from_x(dx, other):
        if other:
            for i in range(2):
                arrived(part(dx, 1, i), p_send.at[dx, i], p_recv.at[dx, i])
        else:
            unit_in(dx, 0)
        unit_to_sibling(dx, other)

    for i, device in enumerate(over):
        send(part(0, 0, i), part(0, 0, i), o_send.at[i], o_recv.at[i], device)
    unit_along_x()
    piece_out(0)
    unit_to_sibling(0, 0)
    for d in far_first(nz):
        send(ints_out.at[d], ints.at[z], z_send.at[1, d], z_recv.at[1, d], at_z(d))
    gets[5].wait()
    for d in far_first(nz):
        send(driver_v.at[:, their_rows(d), :], drv.at[z], z_send.at[2, d], z_recv.at[2, d], at_z(d))
    for p in range(2):
        drv[z, p] = driver_v[p, mine, :]
    ints[z] = ints_out[0]
    for y in (y_own, y_near, y_far):
        y[:, nk] = jnp.zeros((y.shape[0], *y.shape[2:]), f32)

    for d in order[:4]:
        piece_from_z(d)
    part_along_x(0)
    part_along_x(1)
    unit_to_sibling(0, 1)
    for d in order[4:6]:
        piece_from_z(d)
    for d in near_first(nx)[:2]:
        unit_from_x(d, 0)
    for d in order[6:]:
        piece_from_z(d)
    for d in near_first(nx)[2:]:
        unit_from_x(d, 0)

    for d in order:
        arrived(ints.at[(z - d + nz) % nz], z_send.at[1, d], z_recv.at[1, d])
    get_idx = pltpu.make_async_copy(ints, idx, local_sem.at[len(gets)])
    get_idx.start()
    gets[6].wait()
    gets[7].wait()
    for p in range(2):
        own = jnp.broadcast_to(energy_v[0, 0, p : p + 1, :], (width, width))
        turned = jnp.sum(jnp.where(across == down, own, 0.0), axis=1, keepdims=True)
        denom[p] = turned + own + gap_s[0, 0, p]

    def rows_of(h):
        count = h.size // width
        return h[...].reshape(count, width)

    def products(lhs, y, dx, other, far_core):
        o = owner(dx, other, far_core)
        both = jnp.dot(lhs, table[o], preferred_element_type=f32)
        y[:, 2 * o] = both[:, :width].reshape(y.shape[0], rows, width)
        y[:, 2 * o + 1] = both[:, width:].reshape(y.shape[0], rows, width)

    def add_up(pieces, y, first):
        def step(zo, carry):
            for p in range(2):
                total = None if first else acc[zo * 2 + p]
                for i, (d, dy) in enumerate(pieces):
                    place = ((nz - d) % nz) * NY + (NY - dy) % NY
                    for q in range(2):
                        k = idx[zo, p * 2 + q, place]
                        term = y[i * 2 + q, k]
                        total = term if total is None else total + term
                acc[zo * 2 + p] = total
            return carry

        lax.fori_loop(0, nz, step, 0)

    early = [(0, 0), (0, 1)] + [(dx, 0) for dx in near_first(nx)]
    late = [(dx, 1) for dx in near_first(nx)]
    ahead = [0] + order
    pieces_near = [(d, dy) for d in ahead[:near] for dy in range(1, NY)]
    pieces_far = [(d, dy) for d in ahead[near:] for dy in range(1, NY)]

    def pieces_in(pieces):
        for d, dy in pieces:
            arrived(piece(d, dy), y_send.at[d, dy], y_recv.at[d, dy])

    own = rows_of(h_own)
    for n in early:
        products(own, y_own, *n, 0)
    for n in early:
        unit_in(*n, 1)
        products(own, y_own, *n, 1)
    for n in late:
        unit_from_x(*n)
    for n in late:
        products(own, y_own, *n, 0)
    pieces_in(pieces_near)
    beside = rows_of(h_near)
    for far_core in range(2):
        for n in early:
            products(beside, y_near, *n, far_core)
    for n in late:
        products(beside, y_near, *n, 0)
    for n in late:
        unit_in(*n, 1)
        products(own, y_own, *n, 1)
        products(beside, y_near, *n, 1)
    get_idx.wait()
    add_up([(d, 0) for d in ahead], y_own, True)
    add_up(pieces_near, y_near, False)
    pieces_in(pieces_far)
    beyond_rows = rows_of(h_far)
    for far_core in range(2):
        for n in early + late:
            products(beyond_rows, y_far, *n, far_core)
    add_up(pieces_far, y_far, False)

    for d in order:
        arrived(drv.at[(z - d + nz) % nz], z_send.at[2, d], z_recv.at[2, d])
    below = lax.broadcasted_iota(jnp.int32, (rows, width), 0) + z * rows
    aside = lax.broadcasted_iota(jnp.int32, (rows, width), 1)
    squares = jnp.zeros((rows, width), f32)
    for zo in range(nz):
        for p in range(2):
            limit = idx[zo, 4 + p, 0]
            inside = (below < limit) & (aside < limit)
            value = jnp.where(inside, drv[zo, p] + acc[zo * 2 + p], 0.0)
            back[zo, p] = value
            squares = squares + value * value
    squares = jnp.sum(squares, axis=0, keepdims=True)

    def stage_out(i, place, peers, value):
        parts[i, place] = value
        for j, device in enumerate(peers):
            send(parts.at[i, place], parts.at[i, place], m_send.at[i, j], m_recv.at[i, j], device)

    def stage_in(i, places):
        for j, place in reversed(list(enumerate(places))):
            arrived(parts.at[i, place], m_send.at[i, j], m_recv.at[i, j])
        total = parts[i, 0]
        for j in range(1, len(places) + 1):
            total = total + parts[i, j]
        return total

    yy, ny = yh * NL + yl, NY * NL
    stage_out(0, z * NC + core, [at_zc(d, e) for d, e in zc_far], squares)
    for d in far_first(nz):
        send(back.at[(z + d) % nz], home.at[:, mine, :], r_send.at[d], r_recv.at[d], at_z(d))
    for p in range(2):
        home[p, mine, :] = back[z, p]
    total = stage_in(0, [((z - d + nz) % nz) * NC + (core + e) % NC for d, e in zc_far])
    stage_out(1, yy * nx + x, [at_yx(d, e) for d, e in yx_far], total)
    for d in order:
        theirs = pl.ds(pl.multiple_of(((z - d + nz) % nz) * rows, rows), rows)
        arrived(home.at[:, theirs, :], r_send.at[d], r_recv.at[d])
    for p in range(2):
        amps_out[p] = held[p].astype(f32) + home[p] / denom[p]
    for copy in sends:
        copy.wait_send()
    total = stage_in(1, [((yy - d + ny) % ny) * nx + (x - e + nx) % nx for d, e in yx_far])
    rms_out[0, 0] = jnp.max(jnp.sqrt(jnp.full((8, width), jnp.sum(total) / entries, f32)))


def per_device(amps, driver, pattern, domain, virt_energy, pair_gap, integrals):
    width = amps.shape[-1]
    per_block = amps.shape[2]
    nz = lax.axis_size("blk") // NY
    nx = lax.axis_size("col") // (NL * NC)
    rows_of = width // nz
    owners = lax.axis_size("col")
    nk = owners * integrals.shape[0]
    entries = float(lax.axis_size("blk") * owners * per_block * width * width)
    near = 3
    sums = max(nz * NC, NY * NL * nx)
    dma = pltpu.SemaphoreType.DMA
    in_hbm = pl.BlockSpec(memory_space=pltpu.HBM)
    tile = (width, width)
    operands = (
        domain,
        jnp.swapaxes(pattern[0, 0], 1, 2),
        amps[0, 0],
        driver[0, 0],
        virt_energy,
        pair_gap,
        integrals,
    )
    new_amps, rms = pl.pallas_call(
        functools.partial(kernel, nz, nx, entries),
        out_shape=(
            jax.ShapeDtypeStruct((per_block, *tile), jnp.float32),
            jax.ShapeDtypeStruct((1, 1), jnp.float32),
        ),
        in_specs=[in_hbm] * 7,
        out_specs=(pl.BlockSpec(memory_space=pltpu.VMEM), pl.BlockSpec(memory_space=pltpu.SMEM)),
        scratch_shapes=[
            pltpu.SMEM((1, 1, 2), jnp.int32),
            pltpu.SMEM((1, 1, 2), jnp.float32),
            pltpu.VMEM((2, 2, pattern.shape[3]), jnp.int32),
            pltpu.VMEM((1, 1, 2, width), jnp.float32),
            pltpu.VMEM((2, *tile), jnp.bfloat16),
            pltpu.VMEM((2, *tile), jnp.bfloat16),
            pltpu.VMEM((2, *tile), jnp.float32),
            pltpu.VMEM((2, *tile), jnp.float32),
            pltpu.VMEM((owners, width, 2 * width), jnp.bfloat16),
            pltpu.VMEM((nz, 2, rows_of, width), jnp.bfloat16),
            pltpu.VMEM((near, NY - 1, 2, rows_of, width), jnp.bfloat16),
            pltpu.VMEM((nz - near, NY - 1, 2, rows_of, width), jnp.bfloat16),
            pltpu.VMEM((8, width), jnp.int32),
            pltpu.VMEM((nz, 8, width), jnp.int32),
            pltpu.VMEM((nz, 8, width), jnp.int32),
            pltpu.SMEM((nz, 8, width), jnp.int32),
            pltpu.VMEM((nz, 2, rows_of, width), jnp.float32),
            pltpu.VMEM((nz * 2, nk + 1, rows_of, width), jnp.float32),
            pltpu.VMEM((near * (NY - 1) * 2, nk + 1, rows_of, width), jnp.float32),
            pltpu.VMEM(((nz - near) * (NY - 1) * 2, nk + 1, rows_of, width), jnp.float32),
            pltpu.VMEM((nz * 2, rows_of, width), jnp.float32),
            pltpu.VMEM((nz, 2, rows_of, width), jnp.float32),
            pltpu.VMEM((2, *tile), jnp.float32),
            pltpu.VMEM((2, sums, 1, width), jnp.float32),
            dma((9,)),
            dma((3, nz)),
            dma((3, nz)),
            dma((nz, NY)),
            dma((nz, NY)),
            dma((4 * nx,)),
            dma((4 * nx,)),
            dma((2,)),
            dma((2,)),
            dma((nx, 2)),
            dma((nx, 2)),
            dma((nz,)),
            dma((nz,)),
            dma((2, sums)),
            dma((2, sums)),
        ],
        compiler_params=pltpu.CompilerParams(
            collective_id=0, has_side_effects=True, vmem_limit_bytes=40 * 1024 * 1024
        ),
    )(
        *(pltpu.with_memory_space_constraint(a, pltpu.HBM) for a in operands)
    )
    return (new_amps[None, None], rms.reshape(()))


def solution(mesh):
    in_specs = (
        P("blk", "col", None, None, None),
        P("blk", "col", None, None, None),
        P("blk", "col", None, None, None),
        P("blk", "col", None),
        P("blk", "col", None, None),
        P("blk", "col", None),
        P("col", None, None),
    )
    out_specs = (P("blk", "col", None, None, None), P())
    return jax.shard_map(
        per_device, mesh=mesh, in_specs=in_specs, out_specs=out_specs, check_vma=False
    )
```
